32 devices in a mesh: groups: 2 (over y), dp: 4 (over z), net: 4 (over x, core).
Axes of the slice: x: 2, y: 2, z: 4, core: 2. Of those that a mesh axis runs over, the one named last changes fastest.
Arguments:
- part_emb: bfloat16 [8192, 512], P(('groups', 'dp', 'net')), parts along dimension 0, may hold values from -6 to 6
- assign: int32 [8192], P(('groups', 'dp', 'net')), parts along dimension 0, may hold values from 0 to 2047, as said below
- images: bfloat16 [4096, 512], P(('groups', 'dp', 'net')), parts along dimension 0, may hold values from -6 to 6
- negatives: int32 [32, 16], P('groups'), parts along dimension 0, may hold values from 0 to 1, as said below
Outputs:
- pair_loss: float32 [4096], P(('groups', 'dp', 'net')), parts along dimension 0
- net_grad: float32 [4096, 512], P(('groups', 'dp', 'net')), parts along dimension 0
- image_grad: float32 [4096, 512], P(('groups', 'dp', 'net')), parts along dimension 0
The draws below stay inside these ranges and needn't reach their ends.
There are 2 independent parts, one for each index of `groups`. The reference program is written for one: setup_inputs(seed, part) draws one part's arguments, and reference() takes and returns one part's arrays. A program takes and returns all parts, laid end to end along the dimension named above; each array names one. Nothing has to cross between parts.
Inputs may be any that keep to these rules, and one draw needn't show every extreme that they name: Partition i belongs to a pair of its own run: assign[i] // 512 == i // 1024; every pair has one partition or more. An entry 1 marks a column block used as hard negatives of a row block; counts differ widely between row blocks; every row block marks at least one column block of another run; the diagonal block is used whatever its entry.
All inputs are finite; a program needn't handle non-finite values.
Results may differ from the reference program's by a relative error of at most 0.005.
Values may be sent and summed in bfloat16 or wider, within the bound.
A program may use at most 64 MiB of HBM per device.

```python
import jax
import jax.numpy as jnp
from jax import lax

E = 512
BLOCK = 128
PAIR_DP = 512
PART_DP = 1024
PAIRS = 2048
PARTS_SIZE = 4096
NBLK = 16


def make_assign(key):
    base_key = jax.random.fold_in(key, 11)
    run_count = PAIRS // PAIR_DP

    def one_run(run_key, offset):
        fill_key, order_key = jax.random.split(run_key)
        spare_pairs = jax.random.randint(fill_key, (PART_DP - PAIR_DP,), 0, PAIR_DP).astype(jnp.int32)
        local_pairs = jnp.concatenate([jnp.arange(PAIR_DP, dtype=jnp.int32), spare_pairs])
        return jax.random.permutation(order_key, local_pairs) + offset
    run_keys = jax.random.split(base_key, run_count)
    offsets = jnp.arange(run_count, dtype=jnp.int32) * PAIR_DP
    return jax.vmap(one_run)(run_keys, offsets).reshape(PARTS_SIZE).astype(jnp.int32)


def block_shift(key):
    run_count = PAIRS // PAIR_DP
    run_step = jax.random.randint(jax.random.fold_in(key, 31), (), 1, run_count).astype(jnp.int32)
    return run_step * (PAIR_DP // BLOCK)


def bell_rows(key, count):
    return jnp.clip(jax.random.normal(key, (count, E), jnp.float32), -3.5, 3.5)


def draw_assign(key, part):
    return make_assign(key)


def draw_part_emb(key, part):
    assign = make_assign(key)
    latents = bell_rows(jax.random.fold_in(key, 21), PAIRS)
    noise = bell_rows(jax.random.fold_in(key, 22), PARTS_SIZE)
    rows = latents[assign] + 0.5 * noise
    return jnp.clip(rows, -6.0, 6.0).astype(jnp.bfloat16)


def draw_images(key, part):
    shift = block_shift(key)
    columns = jnp.arange(PAIRS, dtype=jnp.int32)
    twin_rows = (columns // BLOCK - shift) % NBLK * BLOCK + columns % BLOCK
    latents = bell_rows(jax.random.fold_in(key, 21), PAIRS)
    noise = bell_rows(jax.random.fold_in(key, 24), PAIRS)
    rows = latents + latents[twin_rows] + 0.5 * noise
    return jnp.clip(rows, -6.0, 6.0).astype(jnp.bfloat16)


def draw_negatives(key, part):
    level_key = jax.random.fold_in(key, 41)
    entry_key = jax.random.fold_in(key, 42)
    density_level = jax.random.randint(level_key, (NBLK, 1), 0, 6).astype(jnp.int32)
    entries = jax.random.randint(entry_key, (NBLK, NBLK), 0, 128).astype(jnp.int32)
    thresholds = jnp.left_shift(jnp.ones((NBLK, 1), jnp.int32), density_level)
    marked = (entries < thresholds).astype(jnp.int32)
    shift = block_shift(key)
    block_ids = jnp.arange(NBLK, dtype=jnp.int32)
    partner = ((block_ids[:, None] + shift) % NBLK == block_ids[None, :]).astype(jnp.int32)
    return jnp.maximum(marked, partner).astype(jnp.int32)


def setup_inputs(seed: int = 0, part: int = 0) -> dict:
    splits = jax.random.split(jax.random.key(seed), 5)
    own_keys = jax.random.split(jax.random.fold_in(splits[4], part), 5)
    return {
        "part_emb": draw_part_emb(jax.random.fold_in(jax.random.fold_in(splits[4], part), 71), part),
        "assign": draw_assign(jax.random.fold_in(jax.random.fold_in(splits[4], part), 71), part),
        "images": draw_images(jax.random.fold_in(jax.random.fold_in(splits[4], part), 71), part),
        "negatives": draw_negatives(jax.random.fold_in(jax.random.fold_in(splits[4], part), 71), part),
    }


logit_scale = 10.0

def unit_rows(matrix):
    squares = lax.optimization_barrier(jnp.sum(matrix * matrix, axis=1, keepdims=True))
    return (matrix * lax.rsqrt(squares + 1e-06)).astype(jnp.bfloat16)

def reference(part_emb, assign, images, negatives):
    pooled = jax.ops.segment_sum(part_emb.astype(jnp.float32), assign, num_segments=PAIRS)
    counted = jax.ops.segment_sum(jnp.ones((PARTS_SIZE,), jnp.float32), assign, num_segments=PAIRS)
    netlist_unit = unit_rows(pooled / counted[:, None]).astype(jnp.float32)
    image_unit = unit_rows(images.astype(jnp.float32)).astype(jnp.float32)
    live_blocks = jnp.maximum(negatives, jnp.eye(NBLK, dtype=jnp.int32)).astype(jnp.float32)

    def row_block(grad_images, block_index):
        first_row = (block_index * BLOCK).astype(jnp.int32)
        net_rows = lax.dynamic_slice_in_dim(netlist_unit, first_row, BLOCK, 0)
        own_images = lax.dynamic_slice_in_dim(image_unit, first_row, BLOCK, 0)
        block_mask = lax.dynamic_slice_in_dim(live_blocks, block_index, 1, 0)[0]
        column_mask = jnp.repeat(block_mask, BLOCK)
        logits = logit_scale * jnp.dot(net_rows, image_unit.T, precision=lax.Precision.HIGHEST)
        weights = jnp.exp(logits) * column_mask[None, :]
        totals = lax.optimization_barrier(jnp.sum(weights, axis=1))
        soft_weights = lax.optimization_barrier((weights / totals[:, None]).astype(jnp.bfloat16)).astype(jnp.float32)
        grad_rows = logit_scale * jnp.dot(soft_weights, image_unit, precision=lax.Precision.HIGHEST) - logit_scale * own_images
        grad_images = grad_images + logit_scale * jnp.dot(soft_weights.T, net_rows, precision=lax.Precision.HIGHEST)
        own_logit = logit_scale * lax.optimization_barrier(jnp.sum(net_rows * own_images, axis=1))
        pair_loss = jnp.log(totals) - own_logit
        return (grad_images, (pair_loss, grad_rows))
    start_grad = jnp.zeros((PAIRS, E), jnp.float32)
    block_ids = jnp.arange(NBLK).astype(jnp.int32)
    grad_images, (pair_loss, net_grad) = lax.scan(row_block, start_grad, block_ids)
    image_grad = grad_images - logit_scale * netlist_unit
    return (pair_loss.reshape(PAIRS), net_grad.reshape(PAIRS, E), image_grad)
```

```python
import functools

import jax
import jax.numpy as jnp
from jax import lax
from jax.experimental import pallas as pl
from jax.experimental.pallas import tpu as pltpu
from jax.sharding import PartitionSpec as P

BLOCK = 128
CHUNKS = 2
LINE = 4
UNIT_CHUNKS = 2
MESH = pl.DeviceIdType.MESH

logit_scale = 10.0


def each(count, body):
    if count <= 4:
        for k in range(1, count):
            body(k)
    else:

        def step(k, carry):
            body(k)
            return carry

        lax.fori_loop(1, count, step, 0)


def line_peer(k, d, size):
    surplus = jnp.maximum(size - 1 - 2 * d, 2 * d - size + 1)
    reach = jnp.minimum(d, size - 1 - d)
    far = jnp.where(2 * d < size - 1, size - 1 - k, k)
    pair = jnp.maximum(k - surplus, 0)
    near = d + (1 - 2 * lax.rem(pair, 2)) * (reach - lax.div(pair, 2))
    return jnp.where(k < surplus, far, near)


def send(src, dst, send_sem, recv_sem, axis, peer):
    return pltpu.make_async_remote_copy(
        src_ref=src,
        dst_ref=dst,
        send_sem=send_sem,
        recv_sem=recv_sem,
        device_id={axis: peer},
        device_id_type=MESH,
    )


def kernel(
    net_size,
    dp_size,
    part_hbm,
    assign_hbm,
    img_hbm,
    neg_hbm,
    loss_ref,
    net_grad_ref,
    img_grad_ref,
    img_raw,
    neg_ref,
    part_all,
    assign_all,
    img_all,
    pooled,
    counted,
    unit,
    weights,
    soft,
    tot_all,
    total,
    row_out,
    row_in,
    col_out,
    col_in,
    local_sem,
    part_s,
    part_r,
    fwd_s,
    asg_s,
    asg_r,
    img_s,
    img_r,
    tot_s,
    tot_r,
    row_s,
    row_r,
    col_s,
    col_r,
    held,
    relay_in,
    relay_s,
    relay_r,
):
    f32, bf16 = jnp.float32, jnp.bfloat16
    rows = img_raw.shape[0]
    part_rows = part_all.shape[1]
    chunk = part_rows // CHUNKS
    pair_dp = rows * net_size
    row_blocks = pair_dp // BLOCK
    own_blocks = rows // BLOCK
    chips = net_size // 2

    n = lax.axis_index("net")
    d = lax.axis_index("dp")
    core = lax.rem(n, 2)
    chip = lax.div(n, 2)
    sibling = n + 1 - 2 * core

    def net_peer(k):
        return lax.rem(n + k, net_size)

    def dp_peer(k):
        return line_peer(k - 1, d, dp_size)

    def chip_peer(k):
        return lax.rem(chip + k, chips)

    img_load = pltpu.make_async_copy(img_hbm, img_raw, local_sem.at[0])
    part_load = pltpu.make_async_copy(part_hbm, part_all.at[n], local_sem.at[1])
    asg_load = pltpu.make_async_copy(assign_hbm, assign_all.at[n], local_sem.at[2])
    neg_load = pltpu.make_async_copy(neg_hbm, neg_ref, local_sem.at[3])

    barrier = pltpu.get_barrier_semaphore()
    each(
        net_size,
        lambda k: pl.semaphore_signal(
            barrier, inc=1, device_id={"net": net_peer(k)}, device_id_type=MESH
        ),
    )
    each(
        dp_size,
        lambda k: pl.semaphore_signal(
            barrier, inc=1, device_id={"dp": dp_peer(k)}, device_id_type=MESH
        ),
    )

    img_load.start()
    part_load.start()
    asg_load.start()
    neg_load.start()
    img_load.wait()
    h = img_raw[...].astype(f32)
    squares = jnp.sum(h * h, axis=1, keepdims=True)
    img_all[d] = (h * lax.rsqrt(squares + 1e-06)).astype(bf16)

    pl.semaphore_wait(barrier, net_size + dp_size - 2)

    def img_copy(k):
        return send(
            img_all.at[d], img_all.at[d], img_s.at[k], img_r.at[d], "dp", dp_peer(k)
        )

    line = dp_size == 4
    at_end = lax.rem(d, 3) == 0
    in_middle = lax.rem(d, 3) > 0

    def img_start(k):
        if line and k == 1:
            pl.when(in_middle)(lambda: img_copy(k).start())
        else:
            img_copy(k).start()

    def img_relay():
        src = dp_peer(1)
        return send(
            img_all.at[src], img_all.at[src], relay_s, img_r.at[src], "dp", 3 * d - 3
        )

    def img_arrival(src):
        return send(img_all.at[src], img_all.at[src], img_s.at[0], img_r.at[src], "dp", d)

    def part_piece(ref, c):
        return ref.at[pl.ds(c * chunk, chunk)]

    def part_cross(k, c):
        return send(
            part_piece(part_hbm, c),
            part_piece(part_all.at[n], c),
            part_s.at[k, c],
            part_r.at[n, c],
            "net",
            chip_peer(k) * 2 + core,
        )

    def part_sibling(c):
        return send(
            part_piece(part_hbm, c),
            part_piece(part_all.at[n], c),
            part_s.at[0, c],
            part_r.at[n, c],
            "net",
            sibling,
        )

    def part_forward(k, c):
        origin = chip_peer(k) * 2 + core
        return send(
            part_piece(part_all.at[origin], c),
            part_piece(part_all.at[origin], c),
            fwd_s.at[k, c],
            part_r.at[origin, c],
            "net",
            sibling,
        )

    def part_arrival(origin, c):
        return send(
            part_piece(part_all.at[origin], c),
            part_piece(part_all.at[origin], c),
            part_s.at[0, c],
            part_r.at[origin, c],
            "net",
            sibling,
        )

    def asg_copy(k):
        return send(
            assign_hbm, assign_all.at[n], asg_s.at[k], asg_r.at[n], "net", net_peer(k)
        )

    def asg_arrival(src):
        return send(
            assign_hbm, assign_all.at[src], asg_s.at[0], asg_r.at[src], "net", sibling
        )

    each(net_size, lambda k: asg_copy(k).start())
    for c in range(CHUNKS):
        each(chips, lambda k: part_cross(k, c).start())
    each(dp_size, img_start)
    for c in range(CHUNKS):
        part_sibling(c).start()

    pair_ids = d * pair_dp + lax.broadcasted_iota(jnp.int32, (pair_dp, part_rows), 0)

    def pool(origin, assigned, first=False):
        member = (assigned == pair_ids).astype(f32)
        sums = jnp.dot(member.astype(bf16), part_all[origin], preferred_element_type=f32)
        counts = jnp.sum(member, axis=1, keepdims=True)
        if first:
            pooled[...] = sums
            counted[...] = counts
        else:
            pooled[...] += sums
            counted[...] += counts

    part_load.wait()
    asg_load.wait()
    pool(n, assign_all[n], first=True)

    def pool_from(origin):
        asg_arrival(origin).wait_recv()
        pool(origin, assign_all[origin])

    for c in range(CHUNKS):
        part_arrival(sibling, c).wait_recv()
    pool_from(sibling)

    def pass_on(k):
        origin = chip_peer(k) * 2 + core
        for c in range(CHUNKS):
            part_arrival(origin, c).wait_recv()
            part_forward(k, c).start()
        pool_from(origin)

    if line:

        @pl.when(in_middle)
        def _():
            img_arrival(dp_peer(1)).wait_recv()
            img_relay().start()

    each(chips, pass_on)

    def pool_passed(k):
        origin = chip_peer(k) * 2 + 1 - core
        for c in range(CHUNKS):
            part_arrival(origin, c).wait_recv()
        pool_from(origin)

    each(chips, pool_passed)

    p = pooled[...]
    cnt = counted[...]
    unit[...] = (
        p * lax.rsqrt(jnp.sum(p * p, axis=1, keepdims=True) + 1e-06 * (cnt * cnt))
    ).astype(bf16)

    def score(src):
        logits = logit_scale * lax.dot_general(
            img_all[src],
            unit[...],
            (((1,), (1,)), ((), ())),
            preferred_element_type=f32,
        )
        w = jnp.exp(logits)
        for q in range(own_blocks):
            column = (src * net_size + n) * own_blocks + q
            marks = []
            for b in range(row_blocks):
                row = d * row_blocks + b
                live = jnp.maximum(neg_ref[row, column], (row == column).astype(jnp.int32))
                marks.append(jnp.full((1, BLOCK), live.astype(f32), f32))
            masked = w[q * BLOCK : (q + 1) * BLOCK] * jnp.concatenate(marks, axis=1)
            start = pl.multiple_of(src * rows + q * BLOCK, BLOCK)
            weights[pl.ds(start, BLOCK), :] = masked
            tot_all[n] += jnp.sum(masked, axis=0, keepdims=True)

    neg_load.wait()
    tot_all[n] = jnp.zeros_like(tot_all[n])
    score(d)

    def score_from(k):
        src = dp_peer(dp_size - k)
        if line and k == dp_size - 1:
            pl.when(at_end)(lambda: img_arrival(src).wait_recv())
        else:
            img_arrival(src).wait_recv()
        score(src)

    each(dp_size, score_from)

    def tot_copy(k):
        return send(
            tot_all.at[n], tot_all.at[n], tot_s.at[k], tot_r.at[n], "net", net_peer(k)
        )

    def tot_arrival(src):
        return send(tot_all.at[src], tot_all.at[src], tot_s.at[0], tot_r.at[src], "net", sibling)

    each(net_size, lambda k: tot_copy(k).start())
    total[...] = tot_all[n]

    own = pl.ds(pl.multiple_of(n * rows, BLOCK), rows)
    own_logits = logit_scale * lax.dot_general(
        img_all[d], unit[own, :], (((1,), (1,)), ((), ())), preferred_element_type=f32
    )
    on_diagonal = lax.broadcasted_iota(jnp.int32, (rows, rows), 0) == lax.broadcasted_iota(
        jnp.int32, (rows, rows), 1
    )
    own_logit = jnp.sum(jnp.where(on_diagonal, own_logits, 0.0), axis=0, keepdims=True)

    def add_total(k):
        src = net_peer(k)
        tot_arrival(src).wait_recv()
        total[...] += tot_all[src]

    each(net_size, add_total)
    inverse = 1.0 / total[...]
    loss_ref[...] = jnp.log(total[:, own]) - own_logit

    def column_grad(src):
        span = pl.ds(pl.multiple_of(src * rows, BLOCK), rows)
        s = (weights[span, :] * inverse).astype(bf16)
        soft[span, :] = s
        return jnp.dot(s, unit[...], preferred_element_type=f32)

    def col_copy(k):
        peer = dp_peer(k)
        return send(
            col_out.at[peer], col_in.at[d], col_s.at[k], col_r.at[d], "dp", peer
        )

    def col_arrival(src):
        return send(col_out.at[src], col_in.at[src], col_s.at[0], col_r.at[src], "dp", d)

    def col_relay():
        return send(
            col_out.at[dp_peer(1)], relay_in, col_s.at[1], relay_r, "dp", dp_peer(dp_size - 1)
        )

    def column_send(k):
        peer = dp_peer(k)
        sums = column_grad(peer)
        if line and k == 1:

            @pl.when(at_end)
            def _():
                col_out[peer] = sums.astype(bf16)
                col_relay().start()

            @pl.when(in_middle)
            def _():
                held[...] = sums

        else:
            col_out[peer] = sums.astype(bf16)
            col_copy(k).start()

    each(dp_size, column_send)
    img_grad_ref[...] = column_grad(d) - unit[own, :].astype(f32)

    every_image = img_all[...].reshape(dp_size * rows, img_all.shape[2])

    def row_grad(dst):
        span = pl.ds(pl.multiple_of(dst * rows, BLOCK), rows)
        return lax.dot_general(
            soft[:, span], every_image, (((0,), (0,)), ((), ())), preferred_element_type=f32
        )

    def row_copy(k):
        peer = net_peer(k)
        return send(row_out.at[peer], row_in.at[n], row_s.at[k], row_r.at[n], "net", peer)

    def row_arrival(src):
        return send(row_out.at[src], row_in.at[src], row_s.at[0], row_r.at[src], "net", sibling)

    def row_send(k):
        peer = net_peer(k)
        row_out[peer] = row_grad(peer).astype(bf16)
        row_copy(k).start()

    each(net_size, row_send)
    net_grad_ref[...] = row_grad(n) - img_all[d].astype(f32)

    if line:

        @pl.when(in_middle)
        def _():
            col_relay().wait_recv()
            far = dp_peer(1)
            col_out[far] = (held[...] + relay_in[...].astype(f32)).astype(bf16)
            col_copy(1).start()

    def row_add(k):
        src = net_peer(k)
        row_arrival(src).wait_recv()
        net_grad_ref[...] += row_in[src].astype(f32)

    each(net_size, row_add)
    net_grad_ref[...] = logit_scale * net_grad_ref[...]

    def col_add(k):
        src = dp_peer(dp_size - k)

        def add():
            col_arrival(src).wait_recv()
            img_grad_ref[...] += col_in[src].astype(f32)

        if line and k == dp_size - 1:
            pl.when(in_middle)(add)
        else:
            add()

    each(dp_size, col_add)
    img_grad_ref[...] = logit_scale * img_grad_ref[...]

    def net_done(k):
        asg_copy(k).wait_send()
        tot_copy(k).wait_send()
        row_copy(k).wait_send()

    def dp_done(k):
        if line and k == 1:

            @pl.when(in_middle)
            def _():
                img_copy(k).wait_send()
                img_relay().wait_send()

            @pl.when(at_end)
            def _():
                col_relay().wait_send()

            pl.when(in_middle)(lambda: col_copy(k).wait_send())
        else:
            img_copy(k).wait_send()
            col_copy(k).wait_send()

    each(net_size, net_done)
    each(dp_size, dp_done)
    for c in range(CHUNKS):
        part_sibling(c).wait_send()

        def chip_done(k):
            part_cross(k, c).wait_send()
            part_forward(k, c).wait_send()

        each(chips, chip_done)


def line_kernel(
    part_hbm,
    assign_hbm,
    img_hbm,
    neg_hbm,
    loss_ref,
    net_grad_ref,
    img_grad_ref,
    img_raw,
    neg_ref,
    part_all,
    assign_all,
    img_all,
    pooled,
    counted,
    unit,
    weights,
    soft,
    tot_all,
    near_unit,
    near_inverse,
    row_other,
    row_own,
    row_out,
    row_in,
    col_out,
    col_in,
    local_sem,
    part_s,
    part_r,
    fwd_s,
    asg_s,
    asg_r,
    img_s,
    img_r,
    tot_s,
    tot_r,
    unit_s,
    unit_r,
    inv_s,
    inv_r,
    row_s,
    row_r,
    col_s,
    col_r,
):
    f32, bf16 = jnp.float32, jnp.bfloat16
    rows = BLOCK
    part_rows = part_all.shape[1]
    chunk = part_rows // CHUNKS
    piece = rows // UNIT_CHUNKS
    pair_dp = LINE * rows
    half = pair_dp // 2

    n = lax.axis_index("net")
    d = lax.axis_index("dp")
    core = lax.rem(n, 2)
    chip = lax.div(n, 2)
    sibling = n + 1 - 2 * core
    cross = (1 - chip) * 2 + core
    diagonal = (1 - chip) * 2 + 1 - core
    side = lax.div(d, 2)
    opposite = 3 - 3 * side
    inner = 2 - side
    is_end = lax.rem(d, 3) == 0
    is_middle = lax.rem(d, 3) > 0

    img_load = pltpu.make_async_copy(img_hbm, img_raw, local_sem.at[0])
    part_load = pltpu.make_async_copy(part_hbm, part_all.at[n], local_sem.at[1])
    asg_load = pltpu.make_async_copy(assign_hbm, assign_all.at[n], local_sem.at[2])
    neg_load = pltpu.make_async_copy(neg_hbm, neg_ref, local_sem.at[3])

    barrier = pltpu.get_barrier_semaphore()
    for k in range(1, LINE):
        pl.semaphore_signal(
            barrier, inc=1, device_id={"dp": lax.rem(d + k, LINE)}, device_id_type=MESH
        )
        pl.semaphore_signal(
            barrier, inc=1, device_id={"net": lax.rem(n + k, LINE)}, device_id_type=MESH
        )

    img_load.start()
    part_load.start()
    asg_load.start()
    neg_load.start()
    img_load.wait()
    h = img_raw[...].astype(f32)
    squares = jnp.sum(h * h, axis=1, keepdims=True)
    img_all[d] = (h * lax.rsqrt(squares + 1e-06)).astype(bf16)

    pl.semaphore_wait(barrier, 2 * (LINE - 1))

    def img_copy(src, k, peer):
        return send(img_all.at[src], img_all.at[src], img_s.at[k], img_r.at[src], "dp", peer)

    def img_sends(act):
        @pl.when(is_end)
        def _():
            act(img_copy(d, 0, inner))
            act(img_copy(d, 1, 1 + side))

        @pl.when(is_middle)
        def _():
            act(img_copy(d, 0, opposite))
            act(img_copy(d, 1, 3 - d))
            act(img_copy(d, 2, 3 * side))

    def img_relay():
        return img_copy(opposite, 3, 3 * side)

    def img_arrival(src):
        return img_copy(src, 0, d)

    def part_piece(ref, c):
        return ref.at[pl.ds(c * chunk, chunk)]

    def part_cross(c):
        return send(
            part_piece(part_hbm, c),
            part_piece(part_all.at[n], c),
            part_s.at[1, c],
            part_r.at[n, c],
            "net",
            cross,
        )

    def part_sibling(c):
        return send(
            part_piece(part_hbm, c),
            part_piece(part_all.at[n], c),
            part_s.at[0, c],
            part_r.at[n, c],
            "net",
            sibling,
        )

    def part_forward(c):
        return send(
            part_piece(part_all.at[cross], c),
            part_piece(part_all.at[cross], c),
            fwd_s.at[c],
            part_r.at[cross, c],
            "net",
            sibling,
        )

    def part_arrival(origin, c):
        return send(
            part_piece(part_all.at[origin], c),
            part_piece(part_all.at[origin], c),
            part_s.at[0, c],
            part_r.at[origin, c],
            "net",
            sibling,
        )

    def asg_copy(k):
        return send(
            assign_hbm,
            assign_all.at[n],
            asg_s.at[k],
            asg_r.at[n],
            "net",
            lax.rem(n + k, LINE),
        )

    def asg_arrival(src):
        return send(
            assign_hbm, assign_all.at[src], asg_s.at[0], asg_r.at[src], "net", sibling
        )

    for k in range(1, LINE):
        asg_copy(k).start()
    for c in range(CHUNKS):
        part_cross(c).start()
    img_sends(lambda copy: copy.start())
    for c in range(CHUNKS):
        part_sibling(c).start()

    pair_ids = d * pair_dp + lax.broadcasted_iota(jnp.int32, (pair_dp, part_rows), 0)

    def pool(origin, first=False):
        member = (assign_all[origin] == pair_ids).astype(f32)
        sums = jnp.dot(member.astype(bf16), part_all[origin], preferred_element_type=f32)
        counts = jnp.sum(member, axis=1, keepdims=True)
        if first:
            pooled[...] = sums
            counted[...] = counts
        else:
            pooled[...] += sums
            counted[...] += counts

    part_load.wait()
    asg_load.wait()
    pool(n, first=True)

    for c in range(CHUNKS):
        part_arrival(sibling, c).wait_recv()
    asg_arrival(sibling).wait_recv()
    pool(sibling)

    for c in range(CHUNKS):
        part_arrival(cross, c).wait_recv()
        part_forward(c).start()
        if c == 0:

            @pl.when(is_middle)
            def _():
                img_arrival(opposite).wait_recv()
                img_relay().start()

    asg_arrival(cross).wait_recv()
    pool(cross)
    for c in range(CHUNKS):
        part_arrival(diagonal, c).wait_recv()
    asg_arrival(diagonal).wait_recv()
    pool(diagonal)

    p = pooled[...]
    cnt = counted[...]
    unit[...] = (
        p * lax.rsqrt(jnp.sum(p * p, axis=1, keepdims=True) + 1e-06 * (cnt * cnt))
    ).astype(bf16)

    own = pl.ds(pl.multiple_of(n * rows, BLOCK), rows)

    def unit_piece(origin, c):
        return pl.ds(pl.multiple_of(origin * rows + c * piece, piece), piece)

    def unit_up(c):
        span = unit_piece(n, c)
        return send(
            unit.at[span], near_unit.at[0, span], unit_s.at[0, c], unit_r.at[0, n, c], "dp", d + 1
        )

    def unit_down(c):
        span = unit_piece(n, c)
        return send(
            unit.at[span], near_unit.at[1, span], unit_s.at[1, c], unit_r.at[1, n, c], "dp", d - 1
        )

    def unit_pass(slot, origin, c, k, peer):
        span = unit_piece(origin, c)
        return send(
            near_unit.at[slot, span],
            near_unit.at[slot, span],
            unit_s.at[k + slot, c],
            unit_r.at[slot, origin, c],
            "net",
            peer,
        )

    def unit_cross(slot, c):
        return unit_pass(slot, n, c, 2, cross)

    def unit_sibling(slot, c):
        return unit_pass(slot, n, c, 4, sibling)

    def unit_forward(slot, c):
        return unit_pass(slot, cross, c, 6, sibling)

    def unit_arrival(slot, origin, c):
        return unit_pass(slot, origin, c, 2, cross)

    below, above = d > 0, d < LINE - 1
    main = jnp.where(is_middle, side, 1 - side)
    spare = 1 - side

    for c in range(UNIT_CHUNKS):
        pl.when(above)(lambda c=c: unit_up(c).start())
        pl.when(below)(lambda c=c: unit_down(c).start())

    def live(row, column):
        mark = jnp.maximum(neg_ref[row, column], (row == column).astype(jnp.int32))
        return jnp.full((1, BLOCK), mark.astype(f32), f32)

    def score(src):
        logits = logit_scale * lax.dot_general(
            img_all[src],
            unit[...],
            (((1,), (1,)), ((), ())),
            preferred_element_type=f32,
        )
        column = src * LINE + n
        marks = [live(d * LINE + b, column) for b in range(LINE)]
        masked = jnp.exp(logits) * jnp.concatenate(marks, axis=1)
        weights[pl.ds(pl.multiple_of(src * rows, BLOCK), rows), :] = masked
        return jnp.sum(masked, axis=0, keepdims=True)

    neg_load.wait()
    first, second = jnp.where(is_end, 1 + side, 3 * side), jnp.where(is_end, inner, 3 - d)
    sums = score(d)
    img_arrival(first).wait_recv()
    sums += score(first)
    img_arrival(second).wait_recv()
    sums += score(second)
    pl.when(is_end)(lambda: img_arrival(opposite).wait_recv())
    sums += score(opposite)
    tot_all[n] = sums

    def tot_copy(k):
        return send(
            tot_all.at[n], tot_all.at[n], tot_s.at[k], tot_r.at[n], "net", lax.rem(n + k, LINE)
        )

    def tot_arrival(src):
        return send(tot_all.at[src], tot_all.at[src], tot_s.at[0], tot_r.at[src], "net", sibling)

    for k in range(1, LINE):
        tot_copy(k).start()

    own_logits = logit_scale * lax.dot_general(
        img_all[d], unit[own, :], (((1,), (1,)), ((), ())), preferred_element_type=f32
    )
    on_diagonal = lax.broadcasted_iota(jnp.int32, (rows, rows), 0) == lax.broadcasted_iota(
        jnp.int32, (rows, rows), 1
    )
    own_logit = jnp.sum(jnp.where(on_diagonal, own_logits, 0.0), axis=0, keepdims=True)

    def take(slot, c):
        unit_arrival(slot, n, c).wait_recv()
        unit_cross(slot, c).start()
        unit_sibling(slot, c).start()

    take(main, 0)

    for src in (sibling, cross, diagonal):
        tot_arrival(src).wait_recv()
    total = tot_all[0] + tot_all[1] + tot_all[2] + tot_all[3]
    near_inverse[2] = 1.0 / total

    def inverse_up():
        return send(
            near_inverse.at[2], near_inverse.at[0], inv_s.at[0], inv_r.at[0], "dp", d + 1
        )

    def inverse_down():
        return send(
            near_inverse.at[2], near_inverse.at[1], inv_s.at[1], inv_r.at[1], "dp", d - 1
        )

    pl.when(above)(lambda: inverse_up().start())
    pl.when(below)(lambda: inverse_down().start())

    def column_grad(src):
        span = pl.ds(pl.multiple_of(src * rows, BLOCK), rows)
        s = (weights[span, :] * near_inverse[2]).astype(bf16)
        soft[span, :] = s
        return jnp.dot(s, unit[...], preferred_element_type=f32)

    def col_copy(k, peer):
        return send(col_out.at[k], col_in.at[k], col_s.at[k], col_r.at[k], "dp", peer)

    far_slot = jnp.where(is_end, 0, 1)

    def far_copy():
        return col_copy(far_slot, opposite)

    col_out[far_slot] = column_grad(opposite).astype(bf16)
    far_copy().start()
    take(main, 1)

    soft[...] = (weights[...] * near_inverse[2]).astype(bf16)

    every_image = img_all[...].reshape(LINE * rows, img_all.shape[2])

    def row_grad(which):
        span = pl.ds(pl.multiple_of(which * half, half), half)
        return lax.dot_general(
            soft[:, span], every_image, (((0,), (0,)), ((), ())), preferred_element_type=f32
        ).reshape(2, rows, img_all.shape[2])

    def row_copy(k, peer):
        return send(row_out.at[k], row_in.at[k], row_s.at[k], row_r.at[k], "net", peer)

    row_other[...] = row_grad(1 - chip)
    row_out[0] = row_other[1 - core].astype(bf16)
    row_copy(0, sibling).start()

    row_own[...] = row_grad(chip)
    row_out[1] = row_own[1 - core].astype(bf16)
    row_copy(1, sibling).start()

    @pl.when(is_middle)
    def _():
        take(spare, 0)
        take(spare, 1)

    row_copy(0, sibling).wait_recv()
    row_out[2] = (row_other[core] + row_in[0].astype(f32)).astype(bf16)
    row_copy(2, cross).start()

    loss_ref[...] = jnp.log(jnp.sum(tot_all[:, :, own], axis=0)) - own_logit
    img_grad_ref[...] = column_grad(d) - unit[own, :].astype(f32)
    row_copy(1, sibling).wait_recv()
    net_grad_ref[...] = row_own[core] - img_all[d].astype(f32) + row_in[1].astype(f32)

    def near_grad(slot, which, owner):
        run = d - 1 + 2 * slot
        span = pl.ds(pl.multiple_of(which * half, half), half)
        theirs = near_unit[slot, span, :]
        logits = logit_scale * lax.dot_general(
            img_all[owner], theirs, (((1,), (1,)), ((), ())), preferred_element_type=f32
        )
        column = owner * LINE + n
        row = run * LINE + which * 2
        marks = jnp.concatenate([live(row, column), live(row + 1, column)], axis=1)
        s = (jnp.exp(logits) * marks * near_inverse[slot, :, span]).astype(bf16)
        return jnp.dot(s, theirs, preferred_element_type=f32)

    def inverse_arrival(slot):
        return send(
            near_inverse.at[2], near_inverse.at[slot], inv_s.at[0], inv_r.at[slot], "dp", d
        )

    def near_own_chip(slot):
        inverse_arrival(slot).wait_recv()
        for c in range(UNIT_CHUNKS):
            unit_arrival(slot, sibling, c).wait_recv()
        img_grad_ref[...] += near_grad(slot, chip, d)

    def pass_on(slot):
        for c in range(UNIT_CHUNKS):
            unit_arrival(slot, cross, c).wait_recv()
            unit_forward(slot, c).start()

    def near_other_chip(slot):
        for c in range(UNIT_CHUNKS):
            unit_arrival(slot, diagonal, c).wait_recv()
        img_grad_ref[...] += near_grad(slot, 1 - chip, d)

    def middle_copy():
        return col_copy(0, 3 - d)

    pass_on(main)
    near_own_chip(main)

    @pl.when(is_middle)
    def _():
        row_other[0] = near_grad(main, chip, 3 - d)


    @pl.when(is_middle)
    def _():
        for c in range(UNIT_CHUNKS):
            unit_arrival(main, diagonal, c).wait_recv()
        col_out[0] = (row_other[0] + near_grad(main, 1 - chip, 3 - d)).astype(bf16)
        middle_copy().start()
        near_own_chip(spare)
        pass_on(spare)
        img_grad_ref[...] += near_grad(main, 1 - chip, d)
        near_other_chip(spare)

    pl.when(is_end)(lambda: near_other_chip(main))

    row_copy(2, cross).wait_recv()
    net_grad_ref[...] = logit_scale * (net_grad_ref[...] + row_in[2].astype(f32))

    @pl.when(is_end)
    def _():
        col_copy(1, d).wait_recv()
        img_grad_ref[...] += col_in[1].astype(f32)

    col_copy(0, d).wait_recv()
    img_grad_ref[...] = logit_scale * (img_grad_ref[...] + col_in[0].astype(f32))

    img_sends(lambda copy: copy.wait_send())
    pl.when(is_middle)(lambda: img_relay().wait_send())
    for c in range(CHUNKS):
        part_cross(c).wait_send()
        part_sibling(c).wait_send()
        part_forward(c).wait_send()
    for k in range(1, LINE):
        asg_copy(k).wait_send()
        tot_copy(k).wait_send()
    row_copy(0, sibling).wait_send()
    row_copy(1, sibling).wait_send()
    row_copy(2, cross).wait_send()
    far_copy().wait_send()
    pl.when(is_middle)(lambda: middle_copy().wait_send())

    @pl.when(above)
    def _():
        inverse_up().wait_send()
        for c in range(UNIT_CHUNKS):
            unit_up(c).wait_send()

    @pl.when(below)
    def _():
        inverse_down().wait_send()
        for c in range(UNIT_CHUNKS):
            unit_down(c).wait_send()

    def near_done(slot):
        for c in range(UNIT_CHUNKS):
            unit_cross(slot, c).wait_send()
            unit_sibling(slot, c).wait_send()
            unit_forward(slot, c).wait_send()

    near_done(main)
    pl.when(is_middle)(lambda: near_done(spare))


def line_scratch(part_rows, width, negatives):
    f32, bf16 = jnp.float32, jnp.bfloat16
    dma = pltpu.SemaphoreType.DMA
    rows, pair_dp = BLOCK, LINE * BLOCK
    return [
        pltpu.VMEM((rows, width), bf16),
        pltpu.SMEM(negatives.shape, jnp.int32),
        pltpu.VMEM((LINE, part_rows, width), bf16),
        pltpu.VMEM((LINE, 1, part_rows), jnp.int32),
        pltpu.VMEM((LINE, rows, width), bf16),
        pltpu.VMEM((pair_dp, width), f32),
        pltpu.VMEM((pair_dp, 1), f32),
        pltpu.VMEM((pair_dp, width), bf16),
        pltpu.VMEM((pair_dp, pair_dp), f32),
        pltpu.VMEM((pair_dp, pair_dp), bf16),
        pltpu.VMEM((LINE, 1, pair_dp), f32),
        pltpu.VMEM((2, pair_dp, width), bf16),
        pltpu.VMEM((3, 1, pair_dp), f32),
        pltpu.VMEM((2, rows, width), f32),
        pltpu.VMEM((2, rows, width), f32),
        pltpu.VMEM((3, rows, width), bf16),
        pltpu.VMEM((3, rows, width), bf16),
        pltpu.VMEM((2, rows, width), bf16),
        pltpu.VMEM((2, rows, width), bf16),
        dma((4,)),
        dma((2, CHUNKS)),
        dma((LINE, CHUNKS)),
        dma((CHUNKS,)),
        dma((LINE,)),
        dma((LINE,)),
        dma((4,)),
        dma((LINE,)),
        dma((LINE,)),
        dma((LINE,)),
        dma((8, UNIT_CHUNKS)),
        dma((2, LINE, UNIT_CHUNKS)),
        dma((2,)),
        dma((2,)),
        dma((3,)),
        dma((3,)),
        dma((2,)),
        dma((2,)),
    ]


def hand_over(loss, net_grad, img_grad, loss_out, net_out, img_out, sem):
    copies = [
        pltpu.make_async_copy(src, dst, sem.at[i])
        for i, (src, dst) in enumerate(
            ((loss, loss_out), (net_grad, net_out), (img_grad, img_out))
        )
    ]
    for copy in copies:
        copy.start()
    for copy in copies:
        copy.wait()


def per_device(part_emb, assign, images, negatives):
    rows, width = images.shape
    part_rows = part_emb.shape[0]
    net_size = lax.axis_size("net")
    dp_size = lax.axis_size("dp")
    chips = net_size // 2
    pair_dp = rows * net_size
    columns = rows * dp_size
    f32, bf16 = jnp.float32, jnp.bfloat16
    dma = pltpu.SemaphoreType.DMA
    vmem = pl.BlockSpec(memory_space=pltpu.VMEM)
    hbm = pl.BlockSpec(memory_space=pltpu.HBM)
    results = (
        jax.ShapeDtypeStruct((1, rows), f32),
        jax.ShapeDtypeStruct((rows, width), f32),
        jax.ShapeDtypeStruct((rows, width), f32),
    )
    scratch = [
        pltpu.VMEM((rows, width), bf16),
        pltpu.SMEM(negatives.shape, jnp.int32),
        pltpu.VMEM((net_size, part_rows, width), bf16),
        pltpu.VMEM((net_size, 1, part_rows), jnp.int32),
        pltpu.VMEM((dp_size, rows, width), bf16),
        pltpu.VMEM((pair_dp, width), f32),
        pltpu.VMEM((pair_dp, 1), f32),
        pltpu.VMEM((pair_dp, width), bf16),
        pltpu.VMEM((columns, pair_dp), f32),
        pltpu.VMEM((columns, pair_dp), bf16),
        pltpu.VMEM((net_size, 1, pair_dp), f32),
        pltpu.VMEM((1, pair_dp), f32),
        pltpu.VMEM((net_size, rows, width), bf16),
        pltpu.VMEM((net_size, rows, width), bf16),
        pltpu.VMEM((dp_size, rows, width), bf16),
        pltpu.VMEM((dp_size, rows, width), bf16),
        dma((4,)),
        dma((chips, CHUNKS)),
        dma((net_size, CHUNKS)),
        dma((chips, CHUNKS)),
        dma((net_size,)),
        dma((net_size,)),
        dma((dp_size,)),
        dma((dp_size,)),
        dma((net_size,)),
        dma((net_size,)),
        dma((net_size,)),
        dma((net_size,)),
        dma((dp_size,)),
        dma((dp_size,)),
        pltpu.VMEM((rows, width), f32),
        pltpu.VMEM((rows, width), bf16),
        dma(()),
        dma(()),
    ]
    body = functools.partial(kernel, net_size, dp_size)
    if net_size == LINE and dp_size == LINE and rows == BLOCK:
        scratch = line_scratch(part_rows, width, negatives)
        body = line_kernel
    loss, net_grad, img_grad = pl.pallas_call(
        body,
        out_shape=results,
        in_specs=[hbm, hbm, hbm, hbm],
        out_specs=(vmem, vmem, vmem),
        scratch_shapes=scratch,
        compiler_params=pltpu.CompilerParams(
            collective_id=0, has_side_effects=True, vmem_limit_bytes=48 * 2**20
        ),
    )(*(
        pltpu.with_memory_space_constraint(array, pltpu.HBM)
        for array in (part_emb, assign.reshape(1, part_rows), images, negatives)
    ))
    loss, net_grad, img_grad = pl.pallas_call(
        hand_over,
        out_shape=results,
        in_specs=[vmem] * 3,
        out_specs=(hbm, hbm, hbm),
        scratch_shapes=[dma((3,))],
    )(*(
        pltpu.with_memory_space_constraint(array, pltpu.VMEM)
        for array in (loss, net_grad, img_grad)
    ))
    return loss.reshape(rows), net_grad, img_grad


def solution(mesh):
    in_specs = (
        P(("groups", "dp", "net"), None),
        P(("groups", "dp", "net")),
        P(("groups", "dp", "net"), None),
        P("groups", None),
    )
    out_specs = (
        P(("groups", "dp", "net")),
        P(("groups", "dp", "net"), None),
        P(("groups", "dp", "net"), None),
    )
    return jax.shard_map(
        per_device, mesh=mesh, in_specs=in_specs, out_specs=out_specs, check_vma=False
    )
```

```python
import functools

import jax
import jax.numpy as jnp
from jax import lax
from jax.experimental import pallas as pl
from jax.experimental.pallas import tpu as pltpu
from jax.sharding import PartitionSpec as P

BLOCK = 128
CHUNKS = 2
LINE = 4
UNIT_CHUNKS = 2
MESH = pl.DeviceIdType.MESH

logit_scale = 10.0


def each(count, body):
    if count <= 4:
        for k in range(1, count):
            body(k)
    else:

        def step(k, carry):
            body(k)
            return carry

        lax.fori_loop(1, count, step, 0)


def line_peer(k, d, size):
    surplus = jnp.maximum(size - 1 - 2 * d, 2 * d - size + 1)
    reach = jnp.minimum(d, size - 1 - d)
    far = jnp.where(2 * d < size - 1, size - 1 - k, k)
    pair = jnp.maximum(k - surplus, 0)
    near = d + (1 - 2 * lax.rem(pair, 2)) * (reach - lax.div(pair, 2))
    return jnp.where(k < surplus, far, near)


def send(src, dst, send_sem, recv_sem, axis, peer):
    return pltpu.make_async_remote_copy(
        src_ref=src,
        dst_ref=dst,
        send_sem=send_sem,
        recv_sem=recv_sem,
        device_id={axis: peer},
        device_id_type=MESH,
    )


def kernel(
    net_size,
    dp_size,
    part_hbm,
    assign_hbm,
    img_hbm,
    neg_hbm,
    loss_ref,
    net_grad_ref,
    img_grad_ref,
    img_raw,
    neg_ref,
    part_all,
    assign_all,
    img_all,
    pooled,
    counted,
    unit,
    weights,
    soft,
    tot_all,
    total,
    row_out,
    row_in,
    col_out,
    col_in,
    local_sem,
    part_s,
    part_r,
    fwd_s,
    asg_s,
    asg_r,
    img_s,
    img_r,
    tot_s,
    tot_r,
    row_s,
    row_r,
    col_s,
    col_r,
    held,
    relay_in,
    relay_s,
    relay_r,
):
    f32, bf16 = jnp.float32, jnp.bfloat16
    rows = img_raw.shape[0]
    part_rows = part_all.shape[1]
    chunk = part_rows // CHUNKS
    pair_dp = rows * net_size
    row_blocks = pair_dp // BLOCK
    own_blocks = rows // BLOCK
    chips = net_size // 2

    n = lax.axis_index("net")
    d = lax.axis_index("dp")
    core = lax.rem(n, 2)
    chip = lax.div(n, 2)
    sibling = n + 1 - 2 * core

    def net_peer(k):
        return lax.rem(n + k, net_size)

    def dp_peer(k):
        return line_peer(k - 1, d, dp_size)

    def chip_peer(k):
        return lax.rem(chip + k, chips)

    img_load = pltpu.make_async_copy(img_hbm, img_raw, local_sem.at[0])
    part_load = pltpu.make_async_copy(part_hbm, part_all.at[n], local_sem.at[1])
    asg_load = pltpu.make_async_copy(assign_hbm, assign_all.at[n], local_sem.at[2])
    neg_load = pltpu.make_async_copy(neg_hbm, neg_ref, local_sem.at[3])

    barrier = pltpu.get_barrier_semaphore()
    each(
        net_size,
        lambda k: pl.semaphore_signal(
            barrier, inc=1, device_id={"net": net_peer(k)}, device_id_type=MESH
        ),
    )
    each(
        dp_size,
        lambda k: pl.semaphore_signal(
            barrier, inc=1, device_id={"dp": dp_peer(k)}, device_id_type=MESH
        ),
    )

    img_load.start()
    part_load.start()
    asg_load.start()
    neg_load.start()
    img_load.wait()
    h = img_raw[...].astype(f32)
    squares = jnp.sum(h * h, axis=1, keepdims=True)
    img_all[d] = (h * lax.rsqrt(squares + 1e-06)).astype(bf16)

    pl.semaphore_wait(barrier, net_size + dp_size - 2)

    def img_copy(k):
        return send(
            img_all.at[d], img_all.at[d], img_s.at[k], img_r.at[d], "dp", dp_peer(k)
        )

    line = dp_size == 4
    at_end = lax.rem(d, 3) == 0
    in_middle = lax.rem(d, 3) > 0

    def img_start(k):
        if line and k == 1:
            pl.when(in_middle)(lambda: img_copy(k).start())
        else:
            img_copy(k).start()

    def img_relay():
        src = dp_peer(1)
        return send(
            img_all.at[src], img_all.at[src], relay_s, img_r.at[src], "dp", 3 * d - 3
        )

    def img_arrival(src):
        return send(img_all.at[src], img_all.at[src], img_s.at[0], img_r.at[src], "dp", d)

    def part_piece(ref, c):
        return ref.at[pl.ds(c * chunk, chunk)]

    def part_cross(k, c):
        return send(
            part_piece(part_hbm, c),
            part_piece(part_all.at[n], c),
            part_s.at[k, c],
            part_r.at[n, c],
            "net",
            chip_peer(k) * 2 + core,
        )

    def part_sibling(c):
        return send(
            part_piece(part_hbm, c),
            part_piece(part_all.at[n], c),
            part_s.at[0, c],
            part_r.at[n, c],
            "net",
            sibling,
        )

    def part_forward(k, c):
        origin = chip_peer(k) * 2 + core
        return send(
            part_piece(part_all.at[origin], c),
            part_piece(part_all.at[origin], c),
            fwd_s.at[k, c],
            part_r.at[origin, c],
            "net",
            sibling,
        )

    def part_arrival(origin, c):
        return send(
            part_piece(part_all.at[origin], c),
            part_piece(part_all.at[origin], c),
            part_s.at[0, c],
            part_r.at[origin, c],
            "net",
            sibling,
        )

    def asg_copy(k):
        return send(
            assign_hbm, assign_all.at[n], asg_s.at[k], asg_r.at[n], "net", net_peer(k)
        )

    def asg_arrival(src):
        return send(
            assign_hbm, assign_all.at[src], asg_s.at[0], asg_r.at[src], "net", sibling
        )

    each(net_size, lambda k: asg_copy(k).start())
    for c in range(CHUNKS):
        each(chips, lambda k: part_cross(k, c).start())
    each(dp_size, img_start)
    for c in range(CHUNKS):
        part_sibling(c).start()

    pair_ids = d * pair_dp + lax.broadcasted_iota(jnp.int32, (pair_dp, part_rows), 0)

    def pool(origin, assigned, first=False):
        member = (assigned == pair_ids).astype(f32)
        sums = jnp.dot(member.astype(bf16), part_all[origin], preferred_element_type=f32)
        counts = jnp.sum(member, axis=1, keepdims=True)
        if first:
            pooled[...] = sums
            counted[...] = counts
        else:
            pooled[...] += sums
            counted[...] += counts

    part_load.wait()
    asg_load.wait()
    pool(n, assign_all[n], first=True)

    def pool_from(origin):
        asg_arrival(origin).wait_recv()
        pool(origin, assign_all[origin])

    for c in range(CHUNKS):
        part_arrival(sibling, c).wait_recv()
    pool_from(sibling)

    def pass_on(k):
        origin = chip_peer(k) * 2 + core
        for c in range(CHUNKS):
            part_arrival(origin, c).wait_recv()
            part_forward(k, c).start()
        pool_from(origin)

    if line:

        @pl.when(in_middle)
        def _():
            img_arrival(dp_peer(1)).wait_recv()
            img_relay().start()

    each(chips, pass_on)

    def pool_passed(k):
        origin = chip_peer(k) * 2 + 1 - core
        for c in range(CHUNKS):
            part_arrival(origin, c).wait_recv()
        pool_from(origin)

    each(chips, pool_passed)

    p = pooled[...]
    cnt = counted[...]
    unit[...] = (
        p * lax.rsqrt(jnp.sum(p * p, axis=1, keepdims=True) + 1e-06 * (cnt * cnt))
    ).astype(bf16)

    def score(src):
        logits = logit_scale * lax.dot_general(
            img_all[src],
            unit[...],
            (((1,), (1,)), ((), ())),
            preferred_element_type=f32,
        )
        w = jnp.exp(logits)
        for q in range(own_blocks):
            column = (src * net_size + n) * own_blocks + q
            marks = []
            for b in range(row_blocks):
                row = d * row_blocks + b
                live = jnp.maximum(neg_ref[row, column], (row == column).astype(jnp.int32))
                marks.append(jnp.full((1, BLOCK), live.astype(f32), f32))
            masked = w[q * BLOCK : (q + 1) * BLOCK] * jnp.concatenate(marks, axis=1)
            start = pl.multiple_of(src * rows + q * BLOCK, BLOCK)
            weights[pl.ds(start, BLOCK), :] = masked
            tot_all[n] += jnp.sum(masked, axis=0, keepdims=True)

    neg_load.wait()
    tot_all[n] = jnp.zeros_like(tot_all[n])
    score(d)

    def score_from(k):
        src = dp_peer(dp_size - k)
        if line and k == dp_size - 1:
            pl.when(at_end)(lambda: img_arrival(src).wait_recv())
        else:
            img_arrival(src).wait_recv()
        score(src)

    each(dp_size, score_from)

    def tot_copy(k):
        return send(
            tot_all.at[n], tot_all.at[n], tot_s.at[k], tot_r.at[n], "net", net_peer(k)
        )

    def tot_arrival(src):
        return send(tot_all.at[src], tot_all.at[src], tot_s.at[0], tot_r.at[src], "net", sibling)

    each(net_size, lambda k: tot_copy(k).start())
    total[...] = tot_all[n]

    own = pl.ds(pl.multiple_of(n * rows, BLOCK), rows)
    own_logits = logit_scale * lax.dot_general(
        img_all[d], unit[own, :], (((1,), (1,)), ((), ())), preferred_element_type=f32
    )
    on_diagonal = lax.broadcasted_iota(jnp.int32, (rows, rows), 0) == lax.broadcasted_iota(
        jnp.int32, (rows, rows), 1
    )
    own_logit = jnp.sum(jnp.where(on_diagonal, own_logits, 0.0), axis=0, keepdims=True)

    def add_total(k):
        src = net_peer(k)
        tot_arrival(src).wait_recv()
        total[...] += tot_all[src]

    each(net_size, add_total)
    inverse = 1.0 / total[...]
    loss_ref[...] = jnp.log(total[:, own]) - own_logit

    def column_grad(src):
        span = pl.ds(pl.multiple_of(src * rows, BLOCK), rows)
        s = (weights[span, :] * inverse).astype(bf16)
        soft[span, :] = s
        return jnp.dot(s, unit[...], preferred_element_type=f32)

    def col_copy(k):
        peer = dp_peer(k)
        return send(
            col_out.at[peer], col_in.at[d], col_s.at[k], col_r.at[d], "dp", peer
        )

    def col_arrival(src):
        return send(col_out.at[src], col_in.at[src], col_s.at[0], col_r.at[src], "dp", d)

    def col_relay():
        return send(
            col_out.at[dp_peer(1)], relay_in, col_s.at[1], relay_r, "dp", dp_peer(dp_size - 1)
        )

    def column_send(k):
        peer = dp_peer(k)
        sums = column_grad(peer)
        if line and k == 1:

            @pl.when(at_end)
            def _():
                col_out[peer] = sums.astype(bf16)
                col_relay().start()

            @pl.when(in_middle)
            def _():
                held[...] = sums

        else:
            col_out[peer] = sums.astype(bf16)
            col_copy(k).start()

    each(dp_size, column_send)
    img_grad_ref[...] = column_grad(d) - unit[own, :].astype(f32)

    every_image = img_all[...].reshape(dp_size * rows, img_all.shape[2])

    def row_grad(dst):
        span = pl.ds(pl.multiple_of(dst * rows, BLOCK), rows)
        return lax.dot_general(
            soft[:, span], every_image, (((0,), (0,)), ((), ())), preferred_element_type=f32
        )

    def row_copy(k):
        peer = net_peer(k)
        return send(row_out.at[peer], row_in.at[n], row_s.at[k], row_r.at[n], "net", peer)

    def row_arrival(src):
        return send(row_out.at[src], row_in.at[src], row_s.at[0], row_r.at[src], "net", sibling)

    def row_send(k):
        peer = net_peer(k)
        row_out[peer] = row_grad(peer).astype(bf16)
        row_copy(k).start()

    each(net_size, row_send)
    net_grad_ref[...] = row_grad(n) - img_all[d].astype(f32)

    if line:

        @pl.when(in_middle)
        def _():
            col_relay().wait_recv()
            far = dp_peer(1)
            col_out[far] = (held[...] + relay_in[...].astype(f32)).astype(bf16)
            col_copy(1).start()

    def row_add(k):
        src = net_peer(k)
        row_arrival(src).wait_recv()
        net_grad_ref[...] += row_in[src].astype(f32)

    each(net_size, row_add)
    net_grad_ref[...] = logit_scale * net_grad_ref[...]

    def col_add(k):
        src = dp_peer(dp_size - k)

        def add():
            col_arrival(src).wait_recv()
            img_grad_ref[...] += col_in[src].astype(f32)

        if line and k == dp_size - 1:
            pl.when(in_middle)(add)
        else:
            add()

    each(dp_size, col_add)
    img_grad_ref[...] = logit_scale * img_grad_ref[...]

    def net_done(k):
        asg_copy(k).wait_send()
        tot_copy(k).wait_send()
        row_copy(k).wait_send()

    def dp_done(k):
        if line and k == 1:

            @pl.when(in_middle)
            def _():
                img_copy(k).wait_send()
                img_relay().wait_send()

            @pl.when(at_end)
            def _():
                col_relay().wait_send()

            pl.when(in_middle)(lambda: col_copy(k).wait_send())
        else:
            img_copy(k).wait_send()
            col_copy(k).wait_send()

    each(net_size, net_done)
    each(dp_size, dp_done)
    for c in range(CHUNKS):
        part_sibling(c).wait_send()

        def chip_done(k):
            part_cross(k, c).wait_send()
            part_forward(k, c).wait_send()

        each(chips, chip_done)


def line_kernel(
    part_hbm,
    assign_hbm,
    img_hbm,
    neg_hbm,
    loss_ref,
    net_grad_ref,
    img_grad_ref,
    img_raw,
    neg_ref,
    part_all,
    assign_all,
    img_all,
    pooled,
    counted,
    unit,
    weights,
    soft,
    tot_all,
    near_unit,
    inverse,
    near_inverse,
    row_other,
    row_own,
    row_out,
    row_in,
    col_out,
    col_in,
    local_sem,
    part_s,
    part_r,
    fwd_s,
    asg_s,
    asg_r,
    img_s,
    img_r,
    tot_s,
    tot_r,
    unit_s,
    unit_r,
    inv_s,
    inv_r,
    row_s,
    row_r,
    col_s,
    col_r,
):
    f32, bf16 = jnp.float32, jnp.bfloat16
    rows = BLOCK
    part_rows = part_all.shape[1]
    chunk = part_rows // CHUNKS
    piece = rows // UNIT_CHUNKS
    pair_dp = LINE * rows
    half = pair_dp // 2

    n = lax.axis_index("net")
    d = lax.axis_index("dp")
    core = lax.rem(n, 2)
    chip = lax.div(n, 2)
    sibling = n + 1 - 2 * core
    cross = (1 - chip) * 2 + core
    diagonal = (1 - chip) * 2 + 1 - core
    side = lax.div(d, 2)
    opposite = 3 - 3 * side
    inner = 2 - side
    is_end = lax.rem(d, 3) == 0
    is_middle = lax.rem(d, 3) > 0

    img_load = pltpu.make_async_copy(img_hbm, img_raw, local_sem.at[0])
    part_load = pltpu.make_async_copy(part_hbm, part_all.at[n], local_sem.at[1])
    asg_load = pltpu.make_async_copy(assign_hbm, assign_all.at[n], local_sem.at[2])
    neg_load = pltpu.make_async_copy(neg_hbm, neg_ref, local_sem.at[3])

    barrier = pltpu.get_barrier_semaphore()
    for k in range(1, LINE):
        pl.semaphore_signal(
            barrier, inc=1, device_id={"dp": lax.rem(d + k, LINE)}, device_id_type=MESH
        )
        pl.semaphore_signal(
            barrier, inc=1, device_id={"net": lax.rem(n + k, LINE)}, device_id_type=MESH
        )

    img_load.start()
    part_load.start()
    asg_load.start()
    neg_load.start()
    img_load.wait()
    h = img_raw[...].astype(f32)
    squares = jnp.sum(h * h, axis=1, keepdims=True)
    img_all[d] = (h * lax.rsqrt(squares + 1e-06)).astype(bf16)

    pl.semaphore_wait(barrier, 2 * (LINE - 1))

    def img_copy(src, k, peer):
        return send(img_all.at[src], img_all.at[src], img_s.at[k], img_r.at[src], "dp", peer)

    def img_sends(act):
        @pl.when(is_end)
        def _():
            act(img_copy(d, 0, inner))
            act(img_copy(d, 1, 1 + side))

        @pl.when(is_middle)
        def _():
            act(img_copy(d, 0, opposite))
            act(img_copy(d, 1, 3 - d))
            act(img_copy(d, 2, 3 * side))

    def img_relay():
        return img_copy(opposite, 3, 3 * side)

    def img_arrival(src):
        return img_copy(src, 0, d)

    def part_piece(ref, c):
        return ref.at[pl.ds(c * chunk, chunk)]

    def part_cross(c):
        return send(
            part_piece(part_all.at[n], c),
            part_piece(part_all.at[n], c),
            part_s.at[1, c],
            part_r.at[n, c],
            "net",
            cross,
        )

    def part_sibling(c):
        return send(
            part_piece(part_all.at[n], c),
            part_piece(part_all.at[n], c),
            part_s.at[0, c],
            part_r.at[n, c],
            "net",
            sibling,
        )

    def part_forward(c):
        return send(
            part_piece(part_all.at[cross], c),
            part_piece(part_all.at[cross], c),
            fwd_s.at[c],
            part_r.at[cross, c],
            "net",
            sibling,
        )

    def part_arrival(origin, c):
        return send(
            part_piece(part_all.at[origin], c),
            part_piece(part_all.at[origin], c),
            part_s.at[0, c],
            part_r.at[origin, c],
            "net",
            sibling,
        )

    def asg_copy(k):
        return send(
            assign_hbm,
            assign_all.at[n],
            asg_s.at[k],
            asg_r.at[n],
            "net",
            lax.rem(n + k, LINE),
        )

    def asg_arrival(src):
        return send(
            assign_hbm, assign_all.at[src], asg_s.at[0], asg_r.at[src], "net", sibling
        )

    part_load.wait()
    for c in range(CHUNKS):
        part_cross(c).start()
    img_sends(lambda copy: copy.start())
    for k in range(1, LINE):
        asg_copy(k).start()
    for c in range(CHUNKS):
        part_sibling(c).start()

    pair_ids = d * pair_dp + lax.broadcasted_iota(jnp.int32, (pair_dp, part_rows), 0)

    def members(origin):
        member = (assign_all[origin] == pair_ids).astype(f32)
        sums = jnp.dot(member.astype(bf16), part_all[origin], preferred_element_type=f32)
        return sums, jnp.sum(member, axis=1, keepdims=True)

    def pool(origin):
        sums, counts = members(origin)
        pooled[...] += sums
        counted[...] += counts

    asg_load.wait()
    pooled[...], counted[...] = members(n)

    for c in range(CHUNKS):
        part_arrival(sibling, c).wait_recv()
    asg_arrival(sibling).wait_recv()
    pool(sibling)

    for c in range(CHUNKS):
        part_arrival(cross, c).wait_recv()
        part_forward(c).start()
        if c == 0:

            @pl.when(is_middle)
            def _():
                img_arrival(opposite).wait_recv()
                img_relay().start()

    asg_arrival(cross).wait_recv()
    pool(cross)
    for c in range(CHUNKS):
        part_arrival(diagonal, c).wait_recv()
    asg_arrival(diagonal).wait_recv()
    sums, counts = members(diagonal)
    p = pooled[...] + sums
    cnt = counted[...] + counts
    unit[...] = (
        p * lax.rsqrt(jnp.sum(p * p, axis=1, keepdims=True) + 1e-06 * (cnt * cnt))
    ).astype(bf16)

    own = pl.ds(pl.multiple_of(n * rows, BLOCK), rows)
    partner = d + 1 - 2 * lax.rem(d, 2)

    def unit_piece(origin, c):
        return pl.ds(pl.multiple_of(origin * rows + c * piece, piece), piece)

    def unit_copy(c):
        span = unit_piece(n, c)
        return send(
            unit.at[span], near_unit.at[span], unit_s.at[0, c], unit_r.at[n, c], "dp", partner
        )

    def unit_pass(origin, c, k, peer):
        span = unit_piece(origin, c)
        return send(
            near_unit.at[span],
            near_unit.at[span],
            unit_s.at[k, c],
            unit_r.at[origin, c],
            "net",
            peer,
        )

    def unit_cross(c):
        return unit_pass(n, c, 1, cross)

    def unit_sibling(c):
        return unit_pass(n, c, 2, sibling)

    def unit_forward(c):
        return unit_pass(cross, c, 3, sibling)

    def unit_arrival(origin, c):
        return unit_pass(origin, c, 1, cross)

    def unit_extra(c):
        span = unit_piece(cross, c)
        return send(
            unit.at[span], near_unit.at[span], unit_s.at[4, c], unit_r.at[cross, c], "dp", partner
        )

    for c in range(UNIT_CHUNKS):
        unit_copy(c).start()

    @pl.when(is_end)
    def _():
        for c in range(UNIT_CHUNKS):
            unit_extra(c).start()

    def live(row, column):
        mark = jnp.maximum(neg_ref[row, column], (row == column).astype(jnp.int32))
        return jnp.full((1, BLOCK), mark.astype(f32), f32)

    def score(start, count):
        span = pl.ds(pl.multiple_of(start * rows, BLOCK), count * rows)
        logits = logit_scale * lax.dot_general(
            img_all[pl.ds(start, count)].reshape(count * rows, img_all.shape[2]),
            unit[...],
            (((1,), (1,)), ((), ())),
            preferred_element_type=f32,
        )
        marks = []
        for q in range(count):
            column = (start + q) * LINE + n
            mark = jnp.concatenate([live(d * LINE + b, column) for b in range(LINE)], axis=1)
            marks.append(jnp.broadcast_to(mark, (rows, pair_dp)))
        masked = jnp.exp(logits) * jnp.concatenate(marks, axis=0)
        weights[span, :] = masked
        return jnp.sum(masked, axis=0, keepdims=True)

    neg_load.wait()
    img_arrival(jnp.where(is_end, 1 + side, 3 * side)).wait_recv()
    img_arrival(jnp.where(is_end, inner, 3 - d)).wait_recv()
    sums = score(side, 3)
    pl.when(is_end)(lambda: img_arrival(opposite).wait_recv())
    tot_all[n] = sums + score(opposite, 1)

    def tot_copy(k):
        return send(
            tot_all.at[n], tot_all.at[n], tot_s.at[k], tot_r.at[n], "net", lax.rem(n + k, LINE)
        )

    def tot_arrival(src):
        return send(tot_all.at[src], tot_all.at[src], tot_s.at[0], tot_r.at[src], "net", sibling)

    for k in range(1, LINE):
        tot_copy(k).start()

    own_logits = logit_scale * lax.dot_general(
        img_all[d], unit[own, :], (((1,), (1,)), ((), ())), preferred_element_type=f32
    )
    on_diagonal = lax.broadcasted_iota(jnp.int32, (rows, rows), 0) == lax.broadcasted_iota(
        jnp.int32, (rows, rows), 1
    )
    own_logit = jnp.sum(jnp.where(on_diagonal, own_logits, 0.0), axis=0, keepdims=True)

    def take(c):
        unit_arrival(n, c).wait_recv()
        pl.when(is_end)(lambda: unit_cross(c).start())
        unit_sibling(c).start()

    take(0)

    for src in (sibling, cross, diagonal):
        tot_arrival(src).wait_recv()
    total = tot_all[0] + tot_all[1] + tot_all[2] + tot_all[3]
    inverse[...] = 1.0 / total

    def inverse_copy():
        return send(inverse, near_inverse, inv_s, inv_r, "dp", partner)

    inverse_copy().start()

    def column_grad(src):
        span = pl.ds(pl.multiple_of(src * rows, BLOCK), rows)
        s = (weights[span, :] * inverse[...]).astype(bf16)
        soft[span, :] = s
        return jnp.dot(s, unit[...], preferred_element_type=f32)

    def col_copy(k, peer):
        return send(col_out.at[k], col_in.at[k], col_s.at[k], col_r.at[k], "dp", peer)

    far_slot = jnp.where(is_end, 0, 1)

    def far_copy():
        return col_copy(far_slot, opposite)

    col_out[far_slot] = column_grad(opposite).astype(bf16)
    far_copy().start()
    take(1)

    soft[...] = (weights[...] * inverse[...]).astype(bf16)

    every_image = img_all[...].reshape(LINE * rows, img_all.shape[2])

    def row_grad(which):
        span = pl.ds(pl.multiple_of(which * half, half), half)
        return lax.dot_general(
            soft[:, span], every_image, (((0,), (0,)), ((), ())), preferred_element_type=f32
        ).reshape(2, rows, img_all.shape[2])

    def row_copy(k, peer):
        return send(row_out.at[k], row_in.at[k], row_s.at[k], row_r.at[k], "net", peer)

    row_other[...] = row_grad(1 - chip)
    row_out[0] = row_other[1 - core].astype(bf16)
    row_copy(0, sibling).start()

    row_own[...] = row_grad(chip)
    row_out[1] = row_own[1 - core].astype(bf16)
    row_copy(1, sibling).start()

    row_copy(0, sibling).wait_recv()
    row_out[2] = (row_other[core] + row_in[0].astype(f32)).astype(bf16)
    row_copy(2, cross).start()

    loss_ref[...] = jnp.log(jnp.sum(tot_all[:, :, own], axis=0)) - own_logit
    img_grad_ref[...] = column_grad(d) - unit[own, :].astype(f32)
    row_copy(1, sibling).wait_recv()
    net_grad_ref[...] = row_own[core] - img_all[d].astype(f32) + row_in[1].astype(f32)

    def near_grad(which, owner):
        span = pl.ds(pl.multiple_of(which * half, half), half)
        theirs = near_unit[span, :]
        logits = logit_scale * lax.dot_general(
            img_all[owner], theirs, (((1,), (1,)), ((), ())), preferred_element_type=f32
        )
        column = owner * LINE + n
        row = partner * LINE + which * 2
        marks = jnp.concatenate([live(row, column), live(row + 1, column)], axis=1)
        s = (jnp.exp(logits) * marks * near_inverse[:, span]).astype(bf16)
        return jnp.dot(s, theirs, preferred_element_type=f32)

    def write_other(sums):
        row_other[0] = sums

    def middle_copy():
        return col_copy(0, 3 - d)

    pl.when(is_middle)(lambda: write_other(column_grad(3 - d)))

    for c in range(UNIT_CHUNKS):
        unit_arrival(cross, c).wait_recv()
        unit_forward(c).start()
    inverse_copy().wait_recv()
    for c in range(UNIT_CHUNKS):
        unit_arrival(sibling, c).wait_recv()
    pl.when(is_middle)(lambda: write_other(row_other[0] + near_grad(chip, 3 - d)))
    img_grad_ref[...] += near_grad(chip, d)
    for c in range(UNIT_CHUNKS):
        unit_arrival(diagonal, c).wait_recv()

    @pl.when(is_middle)
    def _():
        col_out[0] = (row_other[0] + near_grad(1 - chip, 3 - d)).astype(bf16)
        far_copy().wait_send()
        middle_copy().start()

    img_grad_ref[...] += near_grad(1 - chip, d)

    row_copy(2, cross).wait_recv()
    net_grad_ref[...] = logit_scale * (net_grad_ref[...] + row_in[2].astype(f32))

    img_sends(lambda copy: copy.wait_send())
    pl.when(is_middle)(lambda: img_relay().wait_send())
    for c in range(CHUNKS):
        part_cross(c).wait_send()
        part_sibling(c).wait_send()
        part_forward(c).wait_send()
    for k in range(1, LINE):
        asg_copy(k).wait_send()
        tot_copy(k).wait_send()
    row_copy(0, sibling).wait_send()
    row_copy(1, sibling).wait_send()
    row_copy(2, cross).wait_send()

    inverse_copy().wait_send()
    for c in range(UNIT_CHUNKS):
        unit_copy(c).wait_send()
        pl.when(is_end)(lambda c=c: unit_cross(c).wait_send())
        pl.when(is_end)(lambda c=c: unit_extra(c).wait_send())
        unit_sibling(c).wait_send()
        unit_forward(c).wait_send()

    @pl.when(is_end)
    def _():
        col_copy(1, d).wait_recv()
        img_grad_ref[...] += col_in[1].astype(f32)

    col_copy(0, d).wait_recv()
    img_grad_ref[...] = logit_scale * (img_grad_ref[...] + col_in[0].astype(f32))

    pl.when(is_end)(lambda: far_copy().wait_send())
    pl.when(is_middle)(lambda: middle_copy().wait_send())


def line_scratch(part_rows, width, negatives):
    f32, bf16 = jnp.float32, jnp.bfloat16
    dma = pltpu.SemaphoreType.DMA
    rows, pair_dp = BLOCK, LINE * BLOCK
    return [
        pltpu.VMEM((rows, width), bf16),
        pltpu.SMEM(negatives.shape, jnp.int32),
        pltpu.VMEM((LINE, part_rows, width), bf16),
        pltpu.VMEM((LINE, 1, part_rows), jnp.int32),
        pltpu.VMEM((LINE, rows, width), bf16),
        pltpu.VMEM((pair_dp, width), f32),
        pltpu.VMEM((pair_dp, 1), f32),
        pltpu.VMEM((pair_dp, width), bf16),
        pltpu.VMEM((pair_dp, pair_dp), f32),
        pltpu.VMEM((pair_dp, pair_dp), bf16),
        pltpu.VMEM((LINE, 1, pair_dp), f32),
        pltpu.VMEM((pair_dp, width), bf16),
        pltpu.VMEM((1, pair_dp), f32),
        pltpu.VMEM((1, pair_dp), f32),
        pltpu.VMEM((2, rows, width), f32),
        pltpu.VMEM((2, rows, width), f32),
        pltpu.VMEM((3, rows, width), bf16),
        pltpu.VMEM((3, rows, width), bf16),
        pltpu.VMEM((2, rows, width), bf16),
        pltpu.VMEM((2, rows, width), bf16),
        dma((4,)),
        dma((2, CHUNKS)),
        dma((LINE, CHUNKS)),
        dma((CHUNKS,)),
        dma((LINE,)),
        dma((LINE,)),
        dma((4,)),
        dma((LINE,)),
        dma((LINE,)),
        dma((LINE,)),
        dma((5, UNIT_CHUNKS)),
        dma((LINE, UNIT_CHUNKS)),
        dma(()),
        dma(()),
        dma((3,)),
        dma((3,)),
        dma((2,)),
        dma((2,)),
    ]


def hand_over(loss, net_grad, img_grad, loss_out, net_out, img_out, sem):
    copies = [
        pltpu.make_async_copy(src, dst, sem.at[i])
        for i, (src, dst) in enumerate(
            ((loss, loss_out), (net_grad, net_out), (img_grad, img_out))
        )
    ]
    for copy in copies:
        copy.start()
    for copy in copies:
        copy.wait()


def per_device(part_emb, assign, images, negatives):
    rows, width = images.shape
    part_rows = part_emb.shape[0]
    net_size = lax.axis_size("net")
    dp_size = lax.axis_size("dp")
    chips = net_size // 2
    pair_dp = rows * net_size
    columns = rows * dp_size
    f32, bf16 = jnp.float32, jnp.bfloat16
    dma = pltpu.SemaphoreType.DMA
    vmem = pl.BlockSpec(memory_space=pltpu.VMEM)
    hbm = pl.BlockSpec(memory_space=pltpu.HBM)
    results = (
        jax.ShapeDtypeStruct((1, rows), f32),
        jax.ShapeDtypeStruct((rows, width), f32),
        jax.ShapeDtypeStruct((rows, width), f32),
    )
    scratch = [
        pltpu.VMEM((rows, width), bf16),
        pltpu.SMEM(negatives.shape, jnp.int32),
        pltpu.VMEM((net_size, part_rows, width), bf16),
        pltpu.VMEM((net_size, 1, part_rows), jnp.int32),
        pltpu.VMEM((dp_size, rows, width), bf16),
        pltpu.VMEM((pair_dp, width), f32),
        pltpu.VMEM((pair_dp, 1), f32),
        pltpu.VMEM((pair_dp, width), bf16),
        pltpu.VMEM((columns, pair_dp), f32),
        pltpu.VMEM((columns, pair_dp), bf16),
        pltpu.VMEM((net_size, 1, pair_dp), f32),
        pltpu.VMEM((1, pair_dp), f32),
        pltpu.VMEM((net_size, rows, width), bf16),
        pltpu.VMEM((net_size, rows, width), bf16),
        pltpu.VMEM((dp_size, rows, width), bf16),
        pltpu.VMEM((dp_size, rows, width), bf16),
        dma((4,)),
        dma((chips, CHUNKS)),
        dma((net_size, CHUNKS)),
        dma((chips, CHUNKS)),
        dma((net_size,)),
        dma((net_size,)),
        dma((dp_size,)),
        dma((dp_size,)),
        dma((net_size,)),
        dma((net_size,)),
        dma((net_size,)),
        dma((net_size,)),
        dma((dp_size,)),
        dma((dp_size,)),
        pltpu.VMEM((rows, width), f32),
        pltpu.VMEM((rows, width), bf16),
        dma(()),
        dma(()),
    ]
    body = functools.partial(kernel, net_size, dp_size)
    if net_size == LINE and dp_size == LINE and rows == BLOCK:
        scratch = line_scratch(part_rows, width, negatives)
        body = line_kernel
    loss, net_grad, img_grad = pl.pallas_call(
        body,
        out_shape=results,
        in_specs=[hbm, hbm, hbm, hbm],
        out_specs=(vmem, vmem, vmem),
        scratch_shapes=scratch,
        compiler_params=pltpu.CompilerParams(
            collective_id=0, has_side_effects=True, vmem_limit_bytes=48 * 2**20
        ),
    )(*(
        pltpu.with_memory_space_constraint(array, pltpu.HBM)
        for array in (part_emb, assign.reshape(1, part_rows), images, negatives)
    ))
    loss, net_grad, img_grad = pl.pallas_call(
        hand_over,
        out_shape=results,
        in_specs=[vmem] * 3,
        out_specs=(hbm, hbm, hbm),
        scratch_shapes=[dma((3,))],
    )(*(
        pltpu.with_memory_space_constraint(array, pltpu.VMEM)
        for array in (loss, net_grad, img_grad)
    ))
    return loss.reshape(rows), net_grad, img_grad


def solution(mesh):
    in_specs = (
        P(("groups", "dp", "net"), None),
        P(("groups", "dp", "net")),
        P(("groups", "dp", "net"), None),
        P("groups", None),
    )
    out_specs = (
        P(("groups", "dp", "net")),
        P(("groups", "dp", "net"), None),
        P(("groups", "dp", "net"), None),
    )
    return jax.shard_map(
        per_device, mesh=mesh, in_specs=in_specs, out_specs=out_specs, check_vma=False
    )
```

```python
import functools
import math

import jax
import jax.numpy as jnp
from jax import lax
from jax.experimental import pallas as pl
from jax.experimental.pallas import tpu as pltpu
from jax.sharding import PartitionSpec as P

BLOCK = 128
CHUNKS = 2
LINE = 4
UNIT_CHUNKS = 2
MESH = pl.DeviceIdType.MESH

logit_scale = 10.0
logit_scale_2 = logit_scale * math.log2(math.e)


def each(count, body):
    if count <= 4:
        for k in range(1, count):
            body(k)
    else:

        def step(k, carry):
            body(k)
            return carry

        lax.fori_loop(1, count, step, 0)


def line_peer(k, d, size):
    surplus = jnp.maximum(size - 1 - 2 * d, 2 * d - size + 1)
    reach = jnp.minimum(d, size - 1 - d)
    far = jnp.where(2 * d < size - 1, size - 1 - k, k)
    pair = jnp.maximum(k - surplus, 0)
    near = d + (1 - 2 * lax.rem(pair, 2)) * (reach - lax.div(pair, 2))
    return jnp.where(k < surplus, far, near)


def send(src, dst, send_sem, recv_sem, axis, peer):
    return pltpu.make_async_remote_copy(
        src_ref=src,
        dst_ref=dst,
        send_sem=send_sem,
        recv_sem=recv_sem,
        device_id={axis: peer},
        device_id_type=MESH,
    )


def kernel(
    net_size,
    dp_size,
    part_hbm,
    assign_hbm,
    img_hbm,
    neg_hbm,
    loss_ref,
    net_grad_ref,
    img_grad_ref,
    img_raw,
    neg_ref,
    part_all,
    assign_all,
    img_all,
    pooled,
    counted,
    unit,
    weights,
    soft,
    tot_all,
    total,
    row_out,
    row_in,
    col_out,
    col_in,
    local_sem,
    part_s,
    part_r,
    fwd_s,
    asg_s,
    asg_r,
    img_s,
    img_r,
    tot_s,
    tot_r,
    row_s,
    row_r,
    col_s,
    col_r,
    held,
    relay_in,
    relay_s,
    relay_r,
):
    f32, bf16 = jnp.float32, jnp.bfloat16
    rows = img_raw.shape[0]
    part_rows = part_all.shape[1]
    chunk = part_rows // CHUNKS
    pair_dp = rows * net_size
    row_blocks = pair_dp // BLOCK
    own_blocks = rows // BLOCK
    chips = net_size // 2

    n = lax.axis_index("net")
    d = lax.axis_index("dp")
    core = lax.rem(n, 2)
    chip = lax.div(n, 2)
    sibling = n + 1 - 2 * core

    def net_peer(k):
        return lax.rem(n + k, net_size)

    def dp_peer(k):
        return line_peer(k - 1, d, dp_size)

    def chip_peer(k):
        return lax.rem(chip + k, chips)

    img_load = pltpu.make_async_copy(img_hbm, img_raw, local_sem.at[0])
    part_load = pltpu.make_async_copy(part_hbm, part_all.at[n], local_sem.at[1])
    asg_load = pltpu.make_async_copy(assign_hbm, assign_all.at[n], local_sem.at[2])
    neg_load = pltpu.make_async_copy(neg_hbm, neg_ref, local_sem.at[3])

    barrier = pltpu.get_barrier_semaphore()
    each(
        net_size,
        lambda k: pl.semaphore_signal(
            barrier, inc=1, device_id={"net": net_peer(k)}, device_id_type=MESH
        ),
    )
    each(
        dp_size,
        lambda k: pl.semaphore_signal(
            barrier, inc=1, device_id={"dp": dp_peer(k)}, device_id_type=MESH
        ),
    )

    img_load.start()
    part_load.start()
    asg_load.start()
    neg_load.start()
    img_load.wait()
    h = img_raw[...].astype(f32)
    squares = jnp.sum(h * h, axis=1, keepdims=True)
    img_all[d] = (h * lax.rsqrt(squares + 1e-06)).astype(bf16)

    pl.semaphore_wait(barrier, net_size + dp_size - 2)

    def img_copy(k):
        return send(
            img_all.at[d], img_all.at[d], img_s.at[k], img_r.at[d], "dp", dp_peer(k)
        )

    line = dp_size == 4
    at_end = lax.rem(d, 3) == 0
    in_middle = lax.rem(d, 3) > 0

    def img_start(k):
        if line and k == 1:
            pl.when(in_middle)(lambda: img_copy(k).start())
        else:
            img_copy(k).start()

    def img_relay():
        src = dp_peer(1)
        return send(
            img_all.at[src], img_all.at[src], relay_s, img_r.at[src], "dp", 3 * d - 3
        )

    def img_arrival(src):
        return send(img_all.at[src], img_all.at[src], img_s.at[0], img_r.at[src], "dp", d)

    def part_piece(ref, c):
        return ref.at[pl.ds(c * chunk, chunk)]

    def part_cross(k, c):
        return send(
            part_piece(part_hbm, c),
            part_piece(part_all.at[n], c),
            part_s.at[k, c],
            part_r.at[n, c],
            "net",
            chip_peer(k) * 2 + core,
        )

    def part_sibling(c):
        return send(
            part_piece(part_hbm, c),
            part_piece(part_all.at[n], c),
            part_s.at[0, c],
            part_r.at[n, c],
            "net",
            sibling,
        )

    def part_forward(k, c):
        origin = chip_peer(k) * 2 + core
        return send(
            part_piece(part_all.at[origin], c),
            part_piece(part_all.at[origin], c),
            fwd_s.at[k, c],
            part_r.at[origin, c],
            "net",
            sibling,
        )

    def part_arrival(origin, c):
        return send(
            part_piece(part_all.at[origin], c),
            part_piece(part_all.at[origin], c),
            part_s.at[0, c],
            part_r.at[origin, c],
            "net",
            sibling,
        )

    def asg_copy(k):
        return send(
            assign_hbm, assign_all.at[n], asg_s.at[k], asg_r.at[n], "net", net_peer(k)
        )

    def asg_arrival(src):
        return send(
            assign_hbm, assign_all.at[src], asg_s.at[0], asg_r.at[src], "net", sibling
        )

    each(net_size, lambda k: asg_copy(k).start())
    for c in range(CHUNKS):
        each(chips, lambda k: part_cross(k, c).start())
    each(dp_size, img_start)
    for c in range(CHUNKS):
        part_sibling(c).start()

    pair_ids = d * pair_dp + lax.broadcasted_iota(jnp.int32, (pair_dp, part_rows), 0)

    def pool(origin, assigned, first=False):
        member = (assigned == pair_ids).astype(f32)
        sums = jnp.dot(member.astype(bf16), part_all[origin], preferred_element_type=f32)
        counts = jnp.sum(member, axis=1, keepdims=True)
        if first:
            pooled[...] = sums
            counted[...] = counts
        else:
            pooled[...] += sums
            counted[...] += counts

    part_load.wait()
    asg_load.wait()
    pool(n, assign_all[n], first=True)

    def pool_from(origin):
        asg_arrival(origin).wait_recv()
        pool(origin, assign_all[origin])

    for c in range(CHUNKS):
        part_arrival(sibling, c).wait_recv()
    pool_from(sibling)

    def pass_on(k):
        origin = chip_peer(k) * 2 + core
        for c in range(CHUNKS):
            part_arrival(origin, c).wait_recv()
            part_forward(k, c).start()
        pool_from(origin)

    if line:

        @pl.when(in_middle)
        def _():
            img_arrival(dp_peer(1)).wait_recv()
            img_relay().start()

    each(chips, pass_on)

    def pool_passed(k):
        origin = chip_peer(k) * 2 + 1 - core
        for c in range(CHUNKS):
            part_arrival(origin, c).wait_recv()
        pool_from(origin)

    each(chips, pool_passed)

    p = pooled[...]
    cnt = counted[...]
    unit[...] = (
        p * lax.rsqrt(jnp.sum(p * p, axis=1, keepdims=True) + 1e-06 * (cnt * cnt))
    ).astype(bf16)

    def score(src):
        logits = logit_scale * lax.dot_general(
            img_all[src],
            unit[...],
            (((1,), (1,)), ((), ())),
            preferred_element_type=f32,
        )
        w = jnp.exp(logits)
        for q in range(own_blocks):
            column = (src * net_size + n) * own_blocks + q
            marks = []
            for b in range(row_blocks):
                row = d * row_blocks + b
                live = jnp.maximum(neg_ref[row, column], (row == column).astype(jnp.int32))
                marks.append(jnp.full((1, BLOCK), live.astype(f32), f32))
            masked = w[q * BLOCK : (q + 1) * BLOCK] * jnp.concatenate(marks, axis=1)
            start = pl.multiple_of(src * rows + q * BLOCK, BLOCK)
            weights[pl.ds(start, BLOCK), :] = masked
            tot_all[n] += jnp.sum(masked, axis=0, keepdims=True)

    neg_load.wait()
    tot_all[n] = jnp.zeros_like(tot_all[n])
    score(d)

    def score_from(k):
        src = dp_peer(dp_size - k)
        if line and k == dp_size - 1:
            pl.when(at_end)(lambda: img_arrival(src).wait_recv())
        else:
            img_arrival(src).wait_recv()
        score(src)

    each(dp_size, score_from)

    def tot_copy(k):
        return send(
            tot_all.at[n], tot_all.at[n], tot_s.at[k], tot_r.at[n], "net", net_peer(k)
        )

    def tot_arrival(src):
        return send(tot_all.at[src], tot_all.at[src], tot_s.at[0], tot_r.at[src], "net", sibling)

    each(net_size, lambda k: tot_copy(k).start())
    total[...] = tot_all[n]

    own = pl.ds(pl.multiple_of(n * rows, BLOCK), rows)
    own_logits = logit_scale * lax.dot_general(
        img_all[d], unit[own, :], (((1,), (1,)), ((), ())), preferred_element_type=f32
    )
    on_diagonal = lax.broadcasted_iota(jnp.int32, (rows, rows), 0) == lax.broadcasted_iota(
        jnp.int32, (rows, rows), 1
    )
    own_logit = jnp.sum(jnp.where(on_diagonal, own_logits, 0.0), axis=0, keepdims=True)

    def add_total(k):
        src = net_peer(k)
        tot_arrival(src).wait_recv()
        total[...] += tot_all[src]

    each(net_size, add_total)
    inverse = 1.0 / total[...]
    loss_ref[...] = jnp.log(total[:, own]) - own_logit

    def column_grad(src):
        span = pl.ds(pl.multiple_of(src * rows, BLOCK), rows)
        s = (weights[span, :] * inverse).astype(bf16)
        soft[span, :] = s
        return jnp.dot(s, unit[...], preferred_element_type=f32)

    def col_copy(k):
        peer = dp_peer(k)
        return send(
            col_out.at[peer], col_in.at[d], col_s.at[k], col_r.at[d], "dp", peer
        )

    def col_arrival(src):
        return send(col_out.at[src], col_in.at[src], col_s.at[0], col_r.at[src], "dp", d)

    def col_relay():
        return send(
            col_out.at[dp_peer(1)], relay_in, col_s.at[1], relay_r, "dp", dp_peer(dp_size - 1)
        )

    def column_send(k):
        peer = dp_peer(k)
        sums = column_grad(peer)
        if line and k == 1:

            @pl.when(at_end)
            def _():
                col_out[peer] = sums.astype(bf16)
                col_relay().start()

            @pl.when(in_middle)
            def _():
                held[...] = sums

        else:
            col_out[peer] = sums.astype(bf16)
            col_copy(k).start()

    each(dp_size, column_send)
    img_grad_ref[...] = column_grad(d) - unit[own, :].astype(f32)

    every_image = img_all[...].reshape(dp_size * rows, img_all.shape[2])

    def row_grad(dst):
        span = pl.ds(pl.multiple_of(dst * rows, BLOCK), rows)
        return lax.dot_general(
            soft[:, span], every_image, (((0,), (0,)), ((), ())), preferred_element_type=f32
        )

    def row_copy(k):
        peer = net_peer(k)
        return send(row_out.at[peer], row_in.at[n], row_s.at[k], row_r.at[n], "net", peer)

    def row_arrival(src):
        return send(row_out.at[src], row_in.at[src], row_s.at[0], row_r.at[src], "net", sibling)

    def row_send(k):
        peer = net_peer(k)
        row_out[peer] = row_grad(peer).astype(bf16)
        row_copy(k).start()

    each(net_size, row_send)
    net_grad_ref[...] = row_grad(n) - img_all[d].astype(f32)

    if line:

        @pl.when(in_middle)
        def _():
            col_relay().wait_recv()
            far = dp_peer(1)
            col_out[far] = (held[...] + relay_in[...].astype(f32)).astype(bf16)
            col_copy(1).start()

    def row_add(k):
        src = net_peer(k)
        row_arrival(src).wait_recv()
        net_grad_ref[...] += row_in[src].astype(f32)

    each(net_size, row_add)
    net_grad_ref[...] = logit_scale * net_grad_ref[...]

    def col_add(k):
        src = dp_peer(dp_size - k)

        def add():
            col_arrival(src).wait_recv()
            img_grad_ref[...] += col_in[src].astype(f32)

        if line and k == dp_size - 1:
            pl.when(in_middle)(add)
        else:
            add()

    each(dp_size, col_add)
    img_grad_ref[...] = logit_scale * img_grad_ref[...]

    def net_done(k):
        asg_copy(k).wait_send()
        tot_copy(k).wait_send()
        row_copy(k).wait_send()

    def dp_done(k):
        if line and k == 1:

            @pl.when(in_middle)
            def _():
                img_copy(k).wait_send()
                img_relay().wait_send()

            @pl.when(at_end)
            def _():
                col_relay().wait_send()

            pl.when(in_middle)(lambda: col_copy(k).wait_send())
        else:
            img_copy(k).wait_send()
            col_copy(k).wait_send()

    each(net_size, net_done)
    each(dp_size, dp_done)
    for c in range(CHUNKS):
        part_sibling(c).wait_send()

        def chip_done(k):
            part_cross(k, c).wait_send()
            part_forward(k, c).wait_send()

        each(chips, chip_done)


def line_kernel(
    part_hbm,
    assign_hbm,
    img_hbm,
    neg_hbm,
    loss_ref,
    net_grad_ref,
    img_grad_ref,
    img_raw,
    neg_ref,
    part_all,
    assign_all,
    img_all,
    pooled,
    counted,
    unit,
    weights,
    soft,
    tot_all,
    near_unit,
    inverse,
    near_inverse,
    row_other,
    row_own,
    row_out,
    row_in,
    col_out,
    col_in,
    local_sem,
    part_s,
    part_r,
    fwd_s,
    asg_s,
    asg_r,
    img_s,
    img_r,
    tot_s,
    tot_r,
    unit_s,
    unit_r,
    inv_s,
    inv_r,
    row_s,
    row_r,
    col_s,
    col_r,
):
    f32, bf16 = jnp.float32, jnp.bfloat16
    rows = BLOCK
    part_rows = part_all.shape[1]
    chunk = part_rows // CHUNKS
    piece = rows // UNIT_CHUNKS
    pair_dp = LINE * rows
    half = pair_dp // 2

    n = lax.axis_index("net")
    d = lax.axis_index("dp")
    core = lax.rem(n, 2)
    chip = lax.div(n, 2)
    sibling = n + 1 - 2 * core
    cross = (1 - chip) * 2 + core
    diagonal = (1 - chip) * 2 + 1 - core
    side = lax.div(d, 2)
    opposite = 3 - 3 * side
    inner = 2 - side
    is_end = lax.rem(d, 3) == 0
    is_middle = lax.rem(d, 3) > 0

    img_load = pltpu.make_async_copy(img_hbm, img_raw, local_sem.at[0])
    part_load = pltpu.make_async_copy(part_hbm, part_all.at[n], local_sem.at[1])
    asg_load = pltpu.make_async_copy(assign_hbm, assign_all.at[n], local_sem.at[2])
    neg_load = pltpu.make_async_copy(neg_hbm, neg_ref, local_sem.at[3])

    barrier = pltpu.get_barrier_semaphore()
    for k in range(1, LINE):
        pl.semaphore_signal(
            barrier, inc=1, device_id={"dp": lax.rem(d + k, LINE)}, device_id_type=MESH
        )
        pl.semaphore_signal(
            barrier, inc=1, device_id={"net": lax.rem(n + k, LINE)}, device_id_type=MESH
        )

    img_load.start()
    part_load.start()
    asg_load.start()
    neg_load.start()
    img_load.wait()
    h = img_raw[...].astype(f32)
    squares = jnp.sum(h * h, axis=1, keepdims=True)
    img_all[d] = (h * lax.rsqrt(squares + 1e-06)).astype(bf16)

    pl.semaphore_wait(barrier, 2 * (LINE - 1))

    def img_copy(src, k, peer):
        return send(img_all.at[src], img_all.at[src], img_s.at[k], img_r.at[src], "dp", peer)

    def img_sends(act):
        @pl.when(is_end)
        def _():
            act(img_copy(d, 0, inner))
            act(img_copy(d, 1, 1 + side))

        @pl.when(is_middle)
        def _():
            act(img_copy(d, 0, opposite))
            act(img_copy(d, 1, 3 - d))
            act(img_copy(d, 2, 3 * side))

    def img_relay():
        return img_copy(opposite, 3, 3 * side)

    def img_arrival(src):
        return img_copy(src, 0, d)

    def part_piece(ref, c):
        return ref.at[pl.ds(c * chunk, chunk)]

    def part_cross(c):
        return send(
            part_piece(part_all.at[n], c),
            part_piece(part_all.at[n], c),
            part_s.at[1, c],
            part_r.at[n, c],
            "net",
            cross,
        )

    def part_sibling(c):
        return send(
            part_piece(part_all.at[n], c),
            part_piece(part_all.at[n], c),
            part_s.at[0, c],
            part_r.at[n, c],
            "net",
            sibling,
        )

    def part_forward(c):
        return send(
            part_piece(part_all.at[cross], c),
            part_piece(part_all.at[cross], c),
            fwd_s.at[c],
            part_r.at[cross, c],
            "net",
            sibling,
        )

    def part_arrival(origin, c):
        return send(
            part_piece(part_all.at[origin], c),
            part_piece(part_all.at[origin], c),
            part_s.at[0, c],
            part_r.at[origin, c],
            "net",
            sibling,
        )

    def asg_copy(k):
        return send(
            assign_hbm,
            assign_all.at[n],
            asg_s.at[k],
            asg_r.at[n],
            "net",
            lax.rem(n + k, LINE),
        )

    def asg_arrival(src):
        return send(
            assign_hbm, assign_all.at[src], asg_s.at[0], asg_r.at[src], "net", sibling
        )

    part_load.wait()
    for c in range(CHUNKS):
        part_cross(c).start()
    img_sends(lambda copy: copy.start())
    for k in range(1, LINE):
        asg_copy(k).start()
    for c in range(CHUNKS):
        part_sibling(c).start()

    pair_ids = d * pair_dp + lax.broadcasted_iota(jnp.int32, (pair_dp, part_rows), 0)

    def members(origin):
        member = (assign_all[origin] == pair_ids).astype(f32)
        sums = jnp.dot(member.astype(bf16), part_all[origin], preferred_element_type=f32)
        return sums, jnp.sum(member, axis=1, keepdims=True)

    def pool(origin):
        sums, counts = members(origin)
        pooled[...] += sums
        counted[...] += counts

    asg_load.wait()
    pooled[...], counted[...] = members(n)

    for c in range(CHUNKS):
        part_arrival(sibling, c).wait_recv()
    asg_arrival(sibling).wait_recv()
    pool(sibling)

    for c in range(CHUNKS):
        part_arrival(cross, c).wait_recv()
        part_forward(c).start()
        if c == 0:

            @pl.when(is_middle)
            def _():
                img_arrival(opposite).wait_recv()
                img_relay().start()

    asg_arrival(cross).wait_recv()
    pool(cross)
    for c in range(CHUNKS):
        part_arrival(diagonal, c).wait_recv()
    asg_arrival(diagonal).wait_recv()
    own = pl.ds(pl.multiple_of(n * rows, BLOCK), rows)
    partner = d + 1 - 2 * lax.rem(d, 2)

    def unit_piece(origin, c):
        return pl.ds(pl.multiple_of(origin * rows + c * piece, piece), piece)

    def unit_copy(c):
        span = unit_piece(n, c)
        return send(
            unit.at[span], near_unit.at[span], unit_s.at[0, c], unit_r.at[n, c], "dp", partner
        )

    def unit_pass(origin, c, k, peer):
        span = unit_piece(origin, c)
        return send(
            near_unit.at[span],
            near_unit.at[span],
            unit_s.at[k, c],
            unit_r.at[origin, c],
            "net",
            peer,
        )

    def unit_cross(c):
        return unit_pass(n, c, 1, cross)

    def unit_sibling(c):
        return unit_pass(n, c, 2, sibling)

    def unit_forward(c):
        return unit_pass(cross, c, 3, sibling)

    def unit_arrival(origin, c):
        return unit_pass(origin, c, 1, cross)

    def unit_extra(c):
        span = unit_piece(cross, c)
        return send(
            unit.at[span], near_unit.at[span], unit_s.at[4, c], unit_r.at[cross, c], "dp", partner
        )

    pool(diagonal)

    def to_unit(span):
        p, cnt = pooled[span, :], counted[span, :]
        unit[span, :] = (
            p * lax.rsqrt(jnp.sum(p * p, axis=1, keepdims=True) + 1e-06 * (cnt * cnt))
        ).astype(bf16)

    to_unit(own)
    for c in range(UNIT_CHUNKS):
        unit_copy(c).start()
    to_unit(pl.ds(pl.multiple_of(cross * rows, BLOCK), rows))

    @pl.when(is_end)
    def _():
        for c in range(UNIT_CHUNKS):
            unit_extra(c).start()

    to_unit(pl.ds(pl.multiple_of(sibling * rows, BLOCK), rows))
    to_unit(pl.ds(pl.multiple_of(diagonal * rows, BLOCK), rows))

    def live(row, column):
        mark = jnp.maximum(neg_ref[row, column], (row == column).astype(jnp.int32))
        return jnp.full((1, BLOCK), mark.astype(f32), f32)

    def score(start, count):
        span = pl.ds(pl.multiple_of(start * rows, BLOCK), count * rows)
        logits = logit_scale_2 * lax.dot_general(
            img_all[pl.ds(start, count)].reshape(count * rows, img_all.shape[2]),
            unit[...],
            (((1,), (1,)), ((), ())),
            preferred_element_type=f32,
        )
        marks = []
        for q in range(count):
            column = (start + q) * LINE + n
            mark = jnp.concatenate([live(d * LINE + b, column) for b in range(LINE)], axis=1)
            marks.append(jnp.broadcast_to(mark, (rows, pair_dp)))
        masked = jnp.exp2(logits) * jnp.concatenate(marks, axis=0)
        weights[span, :] = masked
        return jnp.sum(masked, axis=0, keepdims=True)

    neg_load.wait()
    img_arrival(jnp.where(is_end, 1 + side, 3 * side)).wait_recv()
    img_arrival(jnp.where(is_end, inner, 3 - d)).wait_recv()
    sums = score(side, 3)
    pl.when(is_end)(lambda: img_arrival(opposite).wait_recv())
    tot_all[n] = sums + score(opposite, 1)

    def tot_copy(k):
        return send(
            tot_all.at[n], tot_all.at[n], tot_s.at[k], tot_r.at[n], "net", lax.rem(n + k, LINE)
        )

    def tot_arrival(src):
        return send(tot_all.at[src], tot_all.at[src], tot_s.at[0], tot_r.at[src], "net", sibling)

    for k in range(1, LINE):
        tot_copy(k).start()

    own_logits = logit_scale * lax.dot_general(
        img_all[d], unit[own, :], (((1,), (1,)), ((), ())), preferred_element_type=f32
    )
    on_diagonal = lax.broadcasted_iota(jnp.int32, (rows, rows), 0) == lax.broadcasted_iota(
        jnp.int32, (rows, rows), 1
    )
    own_logit = jnp.sum(jnp.where(on_diagonal, own_logits, 0.0), axis=0, keepdims=True)

    def take(c):
        unit_arrival(n, c).wait_recv()
        pl.when(is_end)(lambda: unit_cross(c).start())
        unit_sibling(c).start()

    take(0)

    for src in (sibling, cross, diagonal):
        tot_arrival(src).wait_recv()
    total = tot_all[0] + tot_all[1] + tot_all[2] + tot_all[3]
    inverse[...] = 1.0 / total

    def inverse_copy():
        return send(inverse, near_inverse, inv_s, inv_r, "dp", partner)

    inverse_copy().start()

    def column_grad(src):
        span = pl.ds(pl.multiple_of(src * rows, BLOCK), rows)
        s = (weights[span, :] * inverse[...]).astype(bf16)
        soft[span, :] = s
        return jnp.dot(s, unit[...], preferred_element_type=f32)

    def col_copy(k, peer):
        return send(col_out.at[k], col_in.at[k], col_s.at[k], col_r.at[k], "dp", peer)

    far_slot = jnp.where(is_end, 0, 1)

    def far_copy():
        return col_copy(far_slot, opposite)

    col_out[far_slot] = column_grad(opposite).astype(bf16)
    far_copy().start()
    take(1)

    soft[...] = (weights[...] * inverse[...]).astype(bf16)

    every_image = img_all[...].reshape(LINE * rows, img_all.shape[2])

    def row_grad(which):
        span = pl.ds(pl.multiple_of(which * half, half), half)
        return lax.dot_general(
            soft[:, span], every_image, (((0,), (0,)), ((), ())), preferred_element_type=f32
        ).reshape(2, rows, img_all.shape[2])

    def row_copy(k, peer):
        return send(row_out.at[k], row_in.at[k], row_s.at[k], row_r.at[k], "net", peer)

    row_other[...] = row_grad(1 - chip)
    row_out[0] = row_other[1 - core].astype(bf16)
    row_copy(0, sibling).start()

    row_own[...] = row_grad(chip)
    row_out[1] = row_own[1 - core].astype(bf16)
    row_copy(1, sibling).start()

    row_copy(0, sibling).wait_recv()
    row_out[2] = (row_other[core] + row_in[0].astype(f32)).astype(bf16)
    row_copy(2, cross).start()

    loss_ref[...] = jnp.log(jnp.sum(tot_all[:, :, own], axis=0)) - own_logit
    img_grad_ref[...] = column_grad(d) - unit[own, :].astype(f32)
    row_copy(1, sibling).wait_recv()
    net_grad_ref[...] = row_own[core] - img_all[d].astype(f32) + row_in[1].astype(f32)

    def near_grad(which, owner):
        span = pl.ds(pl.multiple_of(which * half, half), half)
        theirs = near_unit[span, :]
        logits = logit_scale_2 * lax.dot_general(
            img_all[owner], theirs, (((1,), (1,)), ((), ())), preferred_element_type=f32
        )
        column = owner * LINE + n
        row = partner * LINE + which * 2
        marks = jnp.concatenate([live(row, column), live(row + 1, column)], axis=1)
        s = (jnp.exp2(logits) * (marks * near_inverse[:, span])).astype(bf16)
        return jnp.dot(s, theirs, preferred_element_type=f32)

    def add_near(which):
        img_grad_ref[...] += near_grad(which, d)

    def write_other(sums):
        row_other[0] = sums

    def middle_copy():
        return col_copy(0, 3 - d)

    pl.when(is_middle)(lambda: write_other(column_grad(3 - d)))

    for c in range(UNIT_CHUNKS):
        unit_arrival(cross, c).wait_recv()
        unit_forward(c).start()
    inverse_copy().wait_recv()
    for c in range(UNIT_CHUNKS):
        unit_arrival(sibling, c).wait_recv()
    pl.when(is_middle)(lambda: write_other(row_other[0] + near_grad(chip, 3 - d)))
    pl.when(is_end)(lambda: add_near(chip))
    for c in range(UNIT_CHUNKS):
        unit_arrival(diagonal, c).wait_recv()

    @pl.when(is_middle)
    def _():
        col_out[0] = (row_other[0] + near_grad(1 - chip, 3 - d)).astype(bf16)
        far_copy().wait_send()
        middle_copy().start()
        add_near(chip)

    add_near(1 - chip)

    row_copy(2, cross).wait_recv()
    net_grad_ref[...] = logit_scale * (net_grad_ref[...] + row_in[2].astype(f32))

    img_sends(lambda copy: copy.wait_send())
    pl.when(is_middle)(lambda: img_relay().wait_send())
    for c in range(CHUNKS):
        part_cross(c).wait_send()
        part_sibling(c).wait_send()
        part_forward(c).wait_send()
    for k in range(1, LINE):
        asg_copy(k).wait_send()
        tot_copy(k).wait_send()
    row_copy(0, sibling).wait_send()
    row_copy(1, sibling).wait_send()
    row_copy(2, cross).wait_send()

    inverse_copy().wait_send()
    for c in range(UNIT_CHUNKS):
        unit_copy(c).wait_send()
        pl.when(is_end)(lambda c=c: unit_cross(c).wait_send())
        pl.when(is_end)(lambda c=c: unit_extra(c).wait_send())
        unit_sibling(c).wait_send()
        unit_forward(c).wait_send()

    @pl.when(is_end)
    def _():
        col_copy(1, d).wait_recv()
        img_grad_ref[...] += col_in[1].astype(f32)

    col_copy(0, d).wait_recv()
    img_grad_ref[...] = logit_scale * (img_grad_ref[...] + col_in[0].astype(f32))

    pl.when(is_end)(lambda: far_copy().wait_send())
    pl.when(is_middle)(lambda: middle_copy().wait_send())


def line_scratch(part_rows, width, negatives):
    f32, bf16 = jnp.float32, jnp.bfloat16
    dma = pltpu.SemaphoreType.DMA
    rows, pair_dp = BLOCK, LINE * BLOCK
    return [
        pltpu.VMEM((rows, width), bf16),
        pltpu.SMEM(negatives.shape, jnp.int32),
        pltpu.VMEM((LINE, part_rows, width), bf16),
        pltpu.VMEM((LINE, 1, part_rows), jnp.int32),
        pltpu.VMEM((LINE, rows, width), bf16),
        pltpu.VMEM((pair_dp, width), f32),
        pltpu.VMEM((pair_dp, 1), f32),
        pltpu.VMEM((pair_dp, width), bf16),
        pltpu.VMEM((pair_dp, pair_dp), f32),
        pltpu.VMEM((pair_dp, pair_dp), bf16),
        pltpu.VMEM((LINE, 1, pair_dp), f32),
        pltpu.VMEM((pair_dp, width), bf16),
        pltpu.VMEM((1, pair_dp), f32),
        pltpu.VMEM((1, pair_dp), f32),
        pltpu.VMEM((2, rows, width), f32),
        pltpu.VMEM((2, rows, width), f32),
        pltpu.VMEM((3, rows, width), bf16),
        pltpu.VMEM((3, rows, width), bf16),
        pltpu.VMEM((2, rows, width), bf16),
        pltpu.VMEM((2, rows, width), bf16),
        dma((4,)),
        dma((2, CHUNKS)),
        dma((LINE, CHUNKS)),
        dma((CHUNKS,)),
        dma((LINE,)),
        dma((LINE,)),
        dma((4,)),
        dma((LINE,)),
        dma((LINE,)),
        dma((LINE,)),
        dma((5, UNIT_CHUNKS)),
        dma((LINE, UNIT_CHUNKS)),
        dma(()),
        dma(()),
        dma((3,)),
        dma((3,)),
        dma((2,)),
        dma((2,)),
    ]


def hand_over(loss, net_grad, img_grad, loss_out, net_out, img_out, sem):
    copies = [
        pltpu.make_async_copy(src, dst, sem.at[i])
        for i, (src, dst) in enumerate(
            ((loss, loss_out), (net_grad, net_out), (img_grad, img_out))
        )
    ]
    for copy in copies:
        copy.start()
    for copy in copies:
        copy.wait()


def per_device(part_emb, assign, images, negatives):
    rows, width = images.shape
    part_rows = part_emb.shape[0]
    net_size = lax.axis_size("net")
    dp_size = lax.axis_size("dp")
    chips = net_size // 2
    pair_dp = rows * net_size
    columns = rows * dp_size
    f32, bf16 = jnp.float32, jnp.bfloat16
    dma = pltpu.SemaphoreType.DMA
    vmem = pl.BlockSpec(memory_space=pltpu.VMEM)
    hbm = pl.BlockSpec(memory_space=pltpu.HBM)
    results = (
        jax.ShapeDtypeStruct((1, rows), f32),
        jax.ShapeDtypeStruct((rows, width), f32),
        jax.ShapeDtypeStruct((rows, width), f32),
    )
    scratch = [
        pltpu.VMEM((rows, width), bf16),
        pltpu.SMEM(negatives.shape, jnp.int32),
        pltpu.VMEM((net_size, part_rows, width), bf16),
        pltpu.VMEM((net_size, 1, part_rows), jnp.int32),
        pltpu.VMEM((dp_size, rows, width), bf16),
        pltpu.VMEM((pair_dp, width), f32),
        pltpu.VMEM((pair_dp, 1), f32),
        pltpu.VMEM((pair_dp, width), bf16),
        pltpu.VMEM((columns, pair_dp), f32),
        pltpu.VMEM((columns, pair_dp), bf16),
        pltpu.VMEM((net_size, 1, pair_dp), f32),
        pltpu.VMEM((1, pair_dp), f32),
        pltpu.VMEM((net_size, rows, width), bf16),
        pltpu.VMEM((net_size, rows, width), bf16),
        pltpu.VMEM((dp_size, rows, width), bf16),
        pltpu.VMEM((dp_size, rows, width), bf16),
        dma((4,)),
        dma((chips, CHUNKS)),
        dma((net_size, CHUNKS)),
        dma((chips, CHUNKS)),
        dma((net_size,)),
        dma((net_size,)),
        dma((dp_size,)),
        dma((dp_size,)),
        dma((net_size,)),
        dma((net_size,)),
        dma((net_size,)),
        dma((net_size,)),
        dma((dp_size,)),
        dma((dp_size,)),
        pltpu.VMEM((rows, width), f32),
        pltpu.VMEM((rows, width), bf16),
        dma(()),
        dma(()),
    ]
    body = functools.partial(kernel, net_size, dp_size)
    if net_size == LINE and dp_size == LINE and rows == BLOCK:
        scratch = line_scratch(part_rows, width, negatives)
        body = line_kernel
    loss, net_grad, img_grad = pl.pallas_call(
        body,
        out_shape=results,
        in_specs=[hbm, hbm, hbm, hbm],
        out_specs=(vmem, vmem, vmem),
        scratch_shapes=scratch,
        compiler_params=pltpu.CompilerParams(
            collective_id=0, has_side_effects=True, vmem_limit_bytes=48 * 2**20
        ),
    )(*(
        pltpu.with_memory_space_constraint(array, pltpu.HBM)
        for array in (part_emb, assign.reshape(1, part_rows), images, negatives)
    ))
    loss, net_grad, img_grad = pl.pallas_call(
        hand_over,
        out_shape=results,
        in_specs=[vmem] * 3,
        out_specs=(hbm, hbm, hbm),
        scratch_shapes=[dma((3,))],
    )(*(
        pltpu.with_memory_space_constraint(array, pltpu.VMEM)
        for array in (loss, net_grad, img_grad)
    ))
    return loss.reshape(rows), net_grad, img_grad


def solution(mesh):
    in_specs = (
        P(("groups", "dp", "net"), None),
        P(("groups", "dp", "net")),
        P(("groups", "dp", "net"), None),
        P("groups", None),
    )
    out_specs = (
        P(("groups", "dp", "net")),
        P(("groups", "dp", "net"), None),
        P(("groups", "dp", "net"), None),
    )
    return jax.shard_map(
        per_device, mesh=mesh, in_specs=in_specs, out_specs=out_specs, check_vma=False
    )
```

```python
import functools
import math

import jax
import jax.numpy as jnp
from jax import lax
from jax.experimental import pallas as pl
from jax.experimental.pallas import tpu as pltpu
from jax.sharding import PartitionSpec as P

BLOCK = 128
CHUNKS = 2
LINE = 4
UNIT_CHUNKS = 2
MESH = pl.DeviceIdType.MESH

logit_scale = 10.0
logit_scale_2 = logit_scale * math.log2(math.e)


def each(count, body):
    if count <= 4:
        for k in range(1, count):
            body(k)
    else:

        def step(k, carry):
            body(k)
            return carry

        lax.fori_loop(1, count, step, 0)


def line_peer(k, d, size):
    surplus = jnp.maximum(size - 1 - 2 * d, 2 * d - size + 1)
    reach = jnp.minimum(d, size - 1 - d)
    far = jnp.where(2 * d < size - 1, size - 1 - k, k)
    pair = jnp.maximum(k - surplus, 0)
    near = d + (1 - 2 * lax.rem(pair, 2)) * (reach - lax.div(pair, 2))
    return jnp.where(k < surplus, far, near)


def send(src, dst, send_sem, recv_sem, axis, peer):
    return pltpu.make_async_remote_copy(
        src_ref=src,
        dst_ref=dst,
        send_sem=send_sem,
        recv_sem=recv_sem,
        device_id={axis: peer},
        device_id_type=MESH,
    )


def kernel(
    net_size,
    dp_size,
    part_hbm,
    assign_hbm,
    img_hbm,
    neg_hbm,
    loss_ref,
    net_grad_ref,
    img_grad_ref,
    img_raw,
    neg_ref,
    part_all,
    assign_all,
    img_all,
    pooled,
    counted,
    unit,
    weights,
    soft,
    tot_all,
    total,
    row_out,
    row_in,
    col_out,
    col_in,
    local_sem,
    part_s,
    part_r,
    fwd_s,
    asg_s,
    asg_r,
    img_s,
    img_r,
    tot_s,
    tot_r,
    row_s,
    row_r,
    col_s,
    col_r,
    held,
    relay_in,
    relay_s,
    relay_r,
):
    f32, bf16 = jnp.float32, jnp.bfloat16
    rows = img_raw.shape[0]
    part_rows = part_all.shape[1]
    chunk = part_rows // CHUNKS
    pair_dp = rows * net_size
    row_blocks = pair_dp // BLOCK
    own_blocks = rows // BLOCK
    chips = net_size // 2

    n = lax.axis_index("net")
    d = lax.axis_index("dp")
    core = lax.rem(n, 2)
    chip = lax.div(n, 2)
    sibling = n + 1 - 2 * core

    def net_peer(k):
        return lax.rem(n + k, net_size)

    def dp_peer(k):
        return line_peer(k - 1, d, dp_size)

    def chip_peer(k):
        return lax.rem(chip + k, chips)

    img_load = pltpu.make_async_copy(img_hbm, img_raw, local_sem.at[0])
    part_load = pltpu.make_async_copy(part_hbm, part_all.at[n], local_sem.at[1])
    asg_load = pltpu.make_async_copy(assign_hbm, assign_all.at[n], local_sem.at[2])
    neg_load = pltpu.make_async_copy(neg_hbm, neg_ref, local_sem.at[3])

    barrier = pltpu.get_barrier_semaphore()
    each(
        net_size,
        lambda k: pl.semaphore_signal(
            barrier, inc=1, device_id={"net": net_peer(k)}, device_id_type=MESH
        ),
    )
    each(
        dp_size,
        lambda k: pl.semaphore_signal(
            barrier, inc=1, device_id={"dp": dp_peer(k)}, device_id_type=MESH
        ),
    )

    img_load.start()
    part_load.start()
    asg_load.start()
    neg_load.start()
    img_load.wait()
    h = img_raw[...].astype(f32)
    squares = jnp.sum(h * h, axis=1, keepdims=True)
    img_all[d] = (h * lax.rsqrt(squares + 1e-06)).astype(bf16)

    pl.semaphore_wait(barrier, net_size + dp_size - 2)

    def img_copy(k):
        return send(
            img_all.at[d], img_all.at[d], img_s.at[k], img_r.at[d], "dp", dp_peer(k)
        )

    line = dp_size == 4
    at_end = lax.rem(d, 3) == 0
    in_middle = lax.rem(d, 3) > 0

    def img_start(k):
        if line and k == 1:
            pl.when(in_middle)(lambda: img_copy(k).start())
        else:
            img_copy(k).start()

    def img_relay():
        src = dp_peer(1)
        return send(
            img_all.at[src], img_all.at[src], relay_s, img_r.at[src], "dp", 3 * d - 3
        )

    def img_arrival(src):
        return send(img_all.at[src], img_all.at[src], img_s.at[0], img_r.at[src], "dp", d)

    def part_piece(ref, c):
        return ref.at[pl.ds(c * chunk, chunk)]

    def part_cross(k, c):
        return send(
            part_piece(part_hbm, c),
            part_piece(part_all.at[n], c),
            part_s.at[k, c],
            part_r.at[n, c],
            "net",
            chip_peer(k) * 2 + core,
        )

    def part_sibling(c):
        return send(
            part_piece(part_hbm, c),
            part_piece(part_all.at[n], c),
            part_s.at[0, c],
            part_r.at[n, c],
            "net",
            sibling,
        )

    def part_forward(k, c):
        origin = chip_peer(k) * 2 + core
        return send(
            part_piece(part_all.at[origin], c),
            part_piece(part_all.at[origin], c),
            fwd_s.at[k, c],
            part_r.at[origin, c],
            "net",
            sibling,
        )

    def part_arrival(origin, c):
        return send(
            part_piece(part_all.at[origin], c),
            part_piece(part_all.at[origin], c),
            part_s.at[0, c],
            part_r.at[origin, c],
            "net",
            sibling,
        )

    def asg_copy(k):
        return send(
            assign_hbm, assign_all.at[n], asg_s.at[k], asg_r.at[n], "net", net_peer(k)
        )

    def asg_arrival(src):
        return send(
            assign_hbm, assign_all.at[src], asg_s.at[0], asg_r.at[src], "net", sibling
        )

    each(net_size, lambda k: asg_copy(k).start())
    for c in range(CHUNKS):
        each(chips, lambda k: part_cross(k, c).start())
    each(dp_size, img_start)
    for c in range(CHUNKS):
        part_sibling(c).start()

    pair_ids = d * pair_dp + lax.broadcasted_iota(jnp.int32, (pair_dp, part_rows), 0)

    def pool(origin, assigned, first=False):
        member = (assigned == pair_ids).astype(f32)
        sums = jnp.dot(member.astype(bf16), part_all[origin], preferred_element_type=f32)
        counts = jnp.sum(member, axis=1, keepdims=True)
        if first:
            pooled[...] = sums
            counted[...] = counts
        else:
            pooled[...] += sums
            counted[...] += counts

    part_load.wait()
    asg_load.wait()
    pool(n, assign_all[n], first=True)

    def pool_from(origin):
        asg_arrival(origin).wait_recv()
        pool(origin, assign_all[origin])

    for c in range(CHUNKS):
        part_arrival(sibling, c).wait_recv()
    pool_from(sibling)

    def pass_on(k):
        origin = chip_peer(k) * 2 + core
        for c in range(CHUNKS):
            part_arrival(origin, c).wait_recv()
            part_forward(k, c).start()
        pool_from(origin)

    if line:

        @pl.when(in_middle)
        def _():
            img_arrival(dp_peer(1)).wait_recv()
            img_relay().start()

    each(chips, pass_on)

    def pool_passed(k):
        origin = chip_peer(k) * 2 + 1 - core
        for c in range(CHUNKS):
            part_arrival(origin, c).wait_recv()
        pool_from(origin)

    each(chips, pool_passed)

    p = pooled[...]
    cnt = counted[...]
    unit[...] = (
        p * lax.rsqrt(jnp.sum(p * p, axis=1, keepdims=True) + 1e-06 * (cnt * cnt))
    ).astype(bf16)

    def score(src):
        logits = logit_scale * lax.dot_general(
            img_all[src],
            unit[...],
            (((1,), (1,)), ((), ())),
            preferred_element_type=f32,
        )
        w = jnp.exp(logits)
        for q in range(own_blocks):
            column = (src * net_size + n) * own_blocks + q
            marks = []
            for b in range(row_blocks):
                row = d * row_blocks + b
                live = jnp.maximum(neg_ref[row, column], (row == column).astype(jnp.int32))
                marks.append(jnp.full((1, BLOCK), live.astype(f32), f32))
            masked = w[q * BLOCK : (q + 1) * BLOCK] * jnp.concatenate(marks, axis=1)
            start = pl.multiple_of(src * rows + q * BLOCK, BLOCK)
            weights[pl.ds(start, BLOCK), :] = masked
            tot_all[n] += jnp.sum(masked, axis=0, keepdims=True)

    neg_load.wait()
    tot_all[n] = jnp.zeros_like(tot_all[n])
    score(d)

    def score_from(k):
        src = dp_peer(dp_size - k)
        if line and k == dp_size - 1:
            pl.when(at_end)(lambda: img_arrival(src).wait_recv())
        else:
            img_arrival(src).wait_recv()
        score(src)

    each(dp_size, score_from)

    def tot_copy(k):
        return send(
            tot_all.at[n], tot_all.at[n], tot_s.at[k], tot_r.at[n], "net", net_peer(k)
        )

    def tot_arrival(src):
        return send(tot_all.at[src], tot_all.at[src], tot_s.at[0], tot_r.at[src], "net", sibling)

    each(net_size, lambda k: tot_copy(k).start())
    total[...] = tot_all[n]

    own = pl.ds(pl.multiple_of(n * rows, BLOCK), rows)
    own_logits = logit_scale * lax.dot_general(
        img_all[d], unit[own, :], (((1,), (1,)), ((), ())), preferred_element_type=f32
    )
    on_diagonal = lax.broadcasted_iota(jnp.int32, (rows, rows), 0) == lax.broadcasted_iota(
        jnp.int32, (rows, rows), 1
    )
    own_logit = jnp.sum(jnp.where(on_diagonal, own_logits, 0.0), axis=0, keepdims=True)

    def add_total(k):
        src = net_peer(k)
        tot_arrival(src).wait_recv()
        total[...] += tot_all[src]

    each(net_size, add_total)
    inverse = 1.0 / total[...]
    loss_ref[...] = jnp.log(total[:, own]) - own_logit

    def column_grad(src):
        span = pl.ds(pl.multiple_of(src * rows, BLOCK), rows)
        s = (weights[span, :] * inverse).astype(bf16)
        soft[span, :] = s
        return jnp.dot(s, unit[...], preferred_element_type=f32)

    def col_copy(k):
        peer = dp_peer(k)
        return send(
            col_out.at[peer], col_in.at[d], col_s.at[k], col_r.at[d], "dp", peer
        )

    def col_arrival(src):
        return send(col_out.at[src], col_in.at[src], col_s.at[0], col_r.at[src], "dp", d)

    def col_relay():
        return send(
            col_out.at[dp_peer(1)], relay_in, col_s.at[1], relay_r, "dp", dp_peer(dp_size - 1)
        )

    def column_send(k):
        peer = dp_peer(k)
        sums = column_grad(peer)
        if line and k == 1:

            @pl.when(at_end)
            def _():
                col_out[peer] = sums.astype(bf16)
                col_relay().start()

            @pl.when(in_middle)
            def _():
                held[...] = sums

        else:
            col_out[peer] = sums.astype(bf16)
            col_copy(k).start()

    each(dp_size, column_send)
    img_grad_ref[...] = column_grad(d) - unit[own, :].astype(f32)

    every_image = img_all[...].reshape(dp_size * rows, img_all.shape[2])

    def row_grad(dst):
        span = pl.ds(pl.multiple_of(dst * rows, BLOCK), rows)
        return lax.dot_general(
            soft[:, span], every_image, (((0,), (0,)), ((), ())), preferred_element_type=f32
        )

    def row_copy(k):
        peer = net_peer(k)
        return send(row_out.at[peer], row_in.at[n], row_s.at[k], row_r.at[n], "net", peer)

    def row_arrival(src):
        return send(row_out.at[src], row_in.at[src], row_s.at[0], row_r.at[src], "net", sibling)

    def row_send(k):
        peer = net_peer(k)
        row_out[peer] = row_grad(peer).astype(bf16)
        row_copy(k).start()

    each(net_size, row_send)
    net_grad_ref[...] = row_grad(n) - img_all[d].astype(f32)

    if line:

        @pl.when(in_middle)
        def _():
            col_relay().wait_recv()
            far = dp_peer(1)
            col_out[far] = (held[...] + relay_in[...].astype(f32)).astype(bf16)
            col_copy(1).start()

    def row_add(k):
        src = net_peer(k)
        row_arrival(src).wait_recv()
        net_grad_ref[...] += row_in[src].astype(f32)

    each(net_size, row_add)
    net_grad_ref[...] = logit_scale * net_grad_ref[...]

    def col_add(k):
        src = dp_peer(dp_size - k)

        def add():
            col_arrival(src).wait_recv()
            img_grad_ref[...] += col_in[src].astype(f32)

        if line and k == dp_size - 1:
            pl.when(in_middle)(add)
        else:
            add()

    each(dp_size, col_add)
    img_grad_ref[...] = logit_scale * img_grad_ref[...]

    def net_done(k):
        asg_copy(k).wait_send()
        tot_copy(k).wait_send()
        row_copy(k).wait_send()

    def dp_done(k):
        if line and k == 1:

            @pl.when(in_middle)
            def _():
                img_copy(k).wait_send()
                img_relay().wait_send()

            @pl.when(at_end)
            def _():
                col_relay().wait_send()

            pl.when(in_middle)(lambda: col_copy(k).wait_send())
        else:
            img_copy(k).wait_send()
            col_copy(k).wait_send()

    each(net_size, net_done)
    each(dp_size, dp_done)
    for c in range(CHUNKS):
        part_sibling(c).wait_send()

        def chip_done(k):
            part_cross(k, c).wait_send()
            part_forward(k, c).wait_send()

        each(chips, chip_done)


def line_kernel(
    part_hbm,
    assign_hbm,
    img_hbm,
    neg_hbm,
    loss_ref,
    net_grad_ref,
    img_grad_ref,
    img_raw,
    neg_ref,
    part_all,
    assign_all,
    img_all,
    pooled,
    counted,
    unit,
    weights,
    soft,
    tot_all,
    near_unit,
    inverse,
    near_inverse,
    row_other,
    row_own,
    row_out,
    row_in,
    col_out,
    col_in,
    local_sem,
    part_s,
    part_r,
    fwd_s,
    asg_s,
    asg_r,
    img_s,
    img_r,
    tot_s,
    tot_r,
    unit_s,
    unit_r,
    inv_s,
    inv_r,
    row_s,
    row_r,
    col_s,
    col_r,
):
    f32, bf16 = jnp.float32, jnp.bfloat16
    rows = BLOCK
    part_rows = part_all.shape[1]
    chunk = part_rows // CHUNKS
    piece = rows // UNIT_CHUNKS
    pair_dp = LINE * rows
    half = pair_dp // 2

    n = lax.axis_index("net")
    d = lax.axis_index("dp")
    core = lax.rem(n, 2)
    chip = lax.div(n, 2)
    sibling = n + 1 - 2 * core
    cross = (1 - chip) * 2 + core
    diagonal = (1 - chip) * 2 + 1 - core
    side = lax.div(d, 2)
    opposite = 3 - 3 * side
    inner = 2 - side
    is_end = lax.rem(d, 3) == 0
    is_middle = lax.rem(d, 3) > 0

    img_load = pltpu.make_async_copy(img_hbm, img_raw, local_sem.at[0])
    part_load = pltpu.make_async_copy(part_hbm, part_all.at[n], local_sem.at[1])
    asg_load = pltpu.make_async_copy(assign_hbm, assign_all.at[n], local_sem.at[2])
    neg_load = pltpu.make_async_copy(neg_hbm, neg_ref, local_sem.at[3])

    barrier = pltpu.get_barrier_semaphore()
    for k in range(1, LINE):
        pl.semaphore_signal(
            barrier, inc=1, device_id={"dp": lax.rem(d + k, LINE)}, device_id_type=MESH
        )
        pl.semaphore_signal(
            barrier, inc=1, device_id={"net": lax.rem(n + k, LINE)}, device_id_type=MESH
        )

    img_load.start()
    part_load.start()
    asg_load.start()
    neg_load.start()
    img_load.wait()
    h = img_raw[...].astype(f32)
    squares = jnp.sum(h * h, axis=1, keepdims=True)
    img_all[d] = (h * lax.rsqrt(squares + 1e-06)).astype(bf16)

    pl.semaphore_wait(barrier, 2 * (LINE - 1))

    def img_copy(src, k, peer):
        return send(img_all.at[src], img_all.at[src], img_s.at[k], img_r.at[src], "dp", peer)

    def img_sends(act):
        @pl.when(is_end)
        def _():
            act(img_copy(d, 0, inner))
            act(img_copy(d, 1, 1 + side))

        @pl.when(is_middle)
        def _():
            act(img_copy(d, 0, opposite))
            act(img_copy(d, 1, 3 - d))
            act(img_copy(d, 2, 3 * side))

    def img_relay():
        return img_copy(opposite, 3, 3 * side)

    def img_arrival(src):
        return img_copy(src, 0, d)

    def part_piece(ref, c):
        return ref.at[pl.ds(c * chunk, chunk)]

    def part_cross(c):
        return send(
            part_piece(part_all.at[n], c),
            part_piece(part_all.at[n], c),
            part_s.at[1, c],
            part_r.at[n, c],
            "net",
            cross,
        )

    def part_sibling(c):
        return send(
            part_piece(part_all.at[n], c),
            part_piece(part_all.at[n], c),
            part_s.at[0, c],
            part_r.at[n, c],
            "net",
            sibling,
        )

    def part_forward(c):
        return send(
            part_piece(part_all.at[cross], c),
            part_piece(part_all.at[cross], c),
            fwd_s.at[c],
            part_r.at[cross, c],
            "net",
            sibling,
        )

    def part_arrival(origin, c):
        return send(
            part_piece(part_all.at[origin], c),
            part_piece(part_all.at[origin], c),
            part_s.at[0, c],
            part_r.at[origin, c],
            "net",
            sibling,
        )

    def asg_copy(k):
        return send(
            assign_hbm,
            assign_all.at[n],
            asg_s.at[k],
            asg_r.at[n],
            "net",
            lax.rem(n + k, LINE),
        )

    def asg_arrival(src):
        return send(
            assign_hbm, assign_all.at[src], asg_s.at[0], asg_r.at[src], "net", sibling
        )

    part_load.wait()
    for c in range(CHUNKS):
        part_cross(c).start()
    img_sends(lambda copy: copy.start())
    for k in range(1, LINE):
        asg_copy(k).start()
    for c in range(CHUNKS):
        part_sibling(c).start()

    pair_ids = d * pair_dp + lax.broadcasted_iota(jnp.int32, (pair_dp, part_rows), 0)

    def members(origin):
        member = (assign_all[origin] == pair_ids).astype(f32)
        sums = jnp.dot(member.astype(bf16), part_all[origin], preferred_element_type=f32)
        return sums, jnp.sum(member, axis=1, keepdims=True)

    def pool(origin):
        sums, counts = members(origin)
        pooled[...] += sums
        counted[...] += counts

    asg_load.wait()
    pooled[...], counted[...] = members(n)

    for c in range(CHUNKS):
        part_arrival(sibling, c).wait_recv()
    asg_arrival(sibling).wait_recv()
    pool(sibling)

    for c in range(CHUNKS):
        part_arrival(cross, c).wait_recv()
        part_forward(c).start()
        if c == 0:

            @pl.when(is_middle)
            def _():
                img_arrival(opposite).wait_recv()
                img_relay().start()

    asg_arrival(cross).wait_recv()
    pool(cross)
    for c in range(CHUNKS):
        part_arrival(diagonal, c).wait_recv()
    asg_arrival(diagonal).wait_recv()
    own = pl.ds(pl.multiple_of(n * rows, BLOCK), rows)
    partner = d + 1 - 2 * lax.rem(d, 2)

    def unit_piece(origin, c):
        return pl.ds(pl.multiple_of(origin * rows + c * piece, piece), piece)

    def unit_copy(c):
        span = unit_piece(n, c)
        return send(
            unit.at[span], near_unit.at[span], unit_s.at[0, c], unit_r.at[n, c], "dp", partner
        )

    def unit_pass(origin, c, k, peer):
        span = unit_piece(origin, c)
        return send(
            near_unit.at[span],
            near_unit.at[span],
            unit_s.at[k, c],
            unit_r.at[origin, c],
            "net",
            peer,
        )

    def unit_cross(c):
        return unit_pass(n, c, 1, cross)

    def unit_sibling(c):
        return unit_pass(n, c, 2, sibling)

    def unit_forward(c):
        return unit_pass(cross, c, 3, sibling)

    def unit_arrival(origin, c):
        return unit_pass(origin, c, 1, cross)

    def unit_extra(c):
        span = unit_piece(cross, c)
        return send(
            unit.at[span], near_unit.at[span], unit_s.at[4, c], unit_r.at[cross, c], "dp", partner
        )

    pool(diagonal)

    def to_unit(span):
        p, cnt = pooled[span, :], counted[span, :]
        unit[span, :] = (
            p * lax.rsqrt(jnp.sum(p * p, axis=1, keepdims=True) + 1e-06 * (cnt * cnt))
        ).astype(bf16)

    to_unit(own)
    for c in range(UNIT_CHUNKS):
        unit_copy(c).start()
    to_unit(pl.ds(pl.multiple_of(cross * rows, BLOCK), rows))

    @pl.when(is_end)
    def _():
        for c in range(UNIT_CHUNKS):
            unit_extra(c).start()

    to_unit(pl.ds(pl.multiple_of(sibling * rows, BLOCK), rows))
    to_unit(pl.ds(pl.multiple_of(diagonal * rows, BLOCK), rows))

    def live(row, column):
        mark = jnp.maximum(neg_ref[row, column], (row == column).astype(jnp.int32))
        return jnp.full((1, BLOCK), mark.astype(f32), f32)

    def score(start, count):
        span = pl.ds(pl.multiple_of(start * rows, BLOCK), count * rows)
        logits = logit_scale_2 * lax.dot_general(
            img_all[pl.ds(start, count)].reshape(count * rows, img_all.shape[2]),
            unit[...],
            (((1,), (1,)), ((), ())),
            preferred_element_type=f32,
        )
        marks = []
        for q in range(count):
            column = (start + q) * LINE + n
            mark = jnp.concatenate([live(d * LINE + b, column) for b in range(LINE)], axis=1)
            marks.append(jnp.broadcast_to(mark, (rows, pair_dp)))
        masked = jnp.exp2(logits) * jnp.concatenate(marks, axis=0)
        weights[span, :] = masked
        return jnp.sum(masked, axis=0, keepdims=True)

    neg_load.wait()
    img_arrival(jnp.where(is_end, 1 + side, 3 * side)).wait_recv()
    img_arrival(jnp.where(is_end, inner, 3 - d)).wait_recv()
    sums = score(side, 3)
    pl.when(is_end)(lambda: img_arrival(opposite).wait_recv())
    tot_all[n] = sums + score(opposite, 1)

    def tot_copy(k):
        return send(
            tot_all.at[n], tot_all.at[n], tot_s.at[k], tot_r.at[n], "net", lax.rem(n + k, LINE)
        )

    def tot_arrival(src):
        return send(tot_all.at[src], tot_all.at[src], tot_s.at[0], tot_r.at[src], "net", sibling)

    for k in range(1, LINE):
        tot_copy(k).start()

    own_logits = logit_scale * lax.dot_general(
        img_all[d], unit[own, :], (((1,), (1,)), ((), ())), preferred_element_type=f32
    )
    on_diagonal = lax.broadcasted_iota(jnp.int32, (rows, rows), 0) == lax.broadcasted_iota(
        jnp.int32, (rows, rows), 1
    )
    own_logit = jnp.sum(jnp.where(on_diagonal, own_logits, 0.0), axis=0, keepdims=True)

    def take(c):
        unit_arrival(n, c).wait_recv()
        pl.when(is_end)(lambda: unit_cross(c).start())
        unit_sibling(c).start()

    pl.when(is_end)(lambda: take(0))

    for src in (sibling, cross, diagonal):
        tot_arrival(src).wait_recv()
    total = tot_all[0] + tot_all[1] + tot_all[2] + tot_all[3]
    inverse[...] = 1.0 / total

    def inverse_copy():
        return send(inverse, near_inverse, inv_s, inv_r, "dp", partner)

    inverse_copy().start()

    def column_grad(src):
        span = pl.ds(pl.multiple_of(src * rows, BLOCK), rows)
        s = (weights[span, :] * inverse[...]).astype(bf16)
        soft[span, :] = s
        return jnp.dot(s, unit[...], preferred_element_type=f32)

    def col_copy(k, peer):
        return send(col_out.at[k], col_in.at[k], col_s.at[k], col_r.at[k], "dp", peer)

    far_slot = jnp.where(is_end, 0, 1)

    def far_copy():
        return col_copy(far_slot, opposite)

    col_out[far_slot] = column_grad(opposite).astype(bf16)
    far_copy().start()
    pl.when(is_middle)(lambda: take(0))
    take(1)

    soft[...] = (weights[...] * inverse[...]).astype(bf16)

    every_image = img_all[...].reshape(LINE * rows, img_all.shape[2])

    def row_grad(which):
        span = pl.ds(pl.multiple_of(which * half, half), half)
        return lax.dot_general(
            soft[:, span], every_image, (((0,), (0,)), ((), ())), preferred_element_type=f32
        ).reshape(2, rows, img_all.shape[2])

    def row_copy(k, peer):
        return send(row_out.at[k], row_in.at[k], row_s.at[k], row_r.at[k], "net", peer)

    row_other[...] = row_grad(1 - chip)
    row_out[0] = row_other[1 - core].astype(bf16)
    row_copy(0, sibling).start()

    row_own[...] = row_grad(chip)
    row_out[1] = row_own[1 - core].astype(bf16)
    row_copy(1, sibling).start()

    row_copy(0, sibling).wait_recv()
    row_out[2] = (row_other[core] + row_in[0].astype(f32)).astype(bf16)
    row_copy(2, cross).start()

    loss_ref[...] = jnp.log(jnp.sum(tot_all[:, :, own], axis=0)) - own_logit
    img_grad_ref[...] = column_grad(d) - unit[own, :].astype(f32)
    row_copy(1, sibling).wait_recv()
    net_grad_ref[...] = row_own[core] - img_all[d].astype(f32) + row_in[1].astype(f32)

    def near_grad(which, owner):
        span = pl.ds(pl.multiple_of(which * half, half), half)
        theirs = near_unit[span, :]
        logits = logit_scale_2 * lax.dot_general(
            img_all[owner], theirs, (((1,), (1,)), ((), ())), preferred_element_type=f32
        )
        column = owner * LINE + n
        row = partner * LINE + which * 2
        marks = jnp.concatenate([live(row, column), live(row + 1, column)], axis=1)
        s = (jnp.exp2(logits) * (marks * near_inverse[:, span])).astype(bf16)
        return jnp.dot(s, theirs, preferred_element_type=f32)

    def add_near(which):
        img_grad_ref[...] += near_grad(which, d)

    def write_other(sums):
        row_other[0] = sums

    def middle_copy():
        return col_copy(0, 3 - d)

    pl.when(is_middle)(lambda: write_other(column_grad(3 - d)))

    for c in range(UNIT_CHUNKS):
        unit_arrival(cross, c).wait_recv()
        unit_forward(c).start()
    inverse_copy().wait_recv()
    for c in range(UNIT_CHUNKS):
        unit_arrival(sibling, c).wait_recv()
    pl.when(is_middle)(lambda: write_other(row_other[0] + near_grad(chip, 3 - d)))
    pl.when(is_end)(lambda: add_near(chip))
    for c in range(UNIT_CHUNKS):
        unit_arrival(diagonal, c).wait_recv()

    @pl.when(is_middle)
    def _():
        col_out[0] = (row_other[0] + near_grad(1 - chip, 3 - d)).astype(bf16)
        far_copy().wait_send()
        middle_copy().start()
        add_near(chip)

    add_near(1 - chip)

    row_copy(2, cross).wait_recv()
    net_grad_ref[...] = logit_scale * (net_grad_ref[...] + row_in[2].astype(f32))

    img_sends(lambda copy: copy.wait_send())
    pl.when(is_middle)(lambda: img_relay().wait_send())
    for c in range(CHUNKS):
        part_cross(c).wait_send()
        part_sibling(c).wait_send()
        part_forward(c).wait_send()
    for k in range(1, LINE):
        asg_copy(k).wait_send()
        tot_copy(k).wait_send()
    row_copy(0, sibling).wait_send()
    row_copy(1, sibling).wait_send()
    row_copy(2, cross).wait_send()

    inverse_copy().wait_send()
    for c in range(UNIT_CHUNKS):
        unit_copy(c).wait_send()
        pl.when(is_end)(lambda c=c: unit_cross(c).wait_send())
        pl.when(is_end)(lambda c=c: unit_extra(c).wait_send())
        unit_sibling(c).wait_send()
        unit_forward(c).wait_send()

    @pl.when(is_end)
    def _():
        col_copy(1, d).wait_recv()
        img_grad_ref[...] += col_in[1].astype(f32)

    col_copy(0, d).wait_recv()
    img_grad_ref[...] = logit_scale * (img_grad_ref[...] + col_in[0].astype(f32))

    pl.when(is_end)(lambda: far_copy().wait_send())
    pl.when(is_middle)(lambda: middle_copy().wait_send())


def line_scratch(part_rows, width, negatives):
    f32, bf16 = jnp.float32, jnp.bfloat16
    dma = pltpu.SemaphoreType.DMA
    rows, pair_dp = BLOCK, LINE * BLOCK
    return [
        pltpu.VMEM((rows, width), bf16),
        pltpu.SMEM(negatives.shape, jnp.int32),
        pltpu.VMEM((LINE, part_rows, width), bf16),
        pltpu.VMEM((LINE, 1, part_rows), jnp.int32),
        pltpu.VMEM((LINE, rows, width), bf16),
        pltpu.VMEM((pair_dp, width), f32),
        pltpu.VMEM((pair_dp, 1), f32),
        pltpu.VMEM((pair_dp, width), bf16),
        pltpu.VMEM((pair_dp, pair_dp), f32),
        pltpu.VMEM((pair_dp, pair_dp), bf16),
        pltpu.VMEM((LINE, 1, pair_dp), f32),
        pltpu.VMEM((pair_dp, width), bf16),
        pltpu.VMEM((1, pair_dp), f32),
        pltpu.VMEM((1, pair_dp), f32),
        pltpu.VMEM((2, rows, width), f32),
        pltpu.VMEM((2, rows, width), f32),
        pltpu.VMEM((3, rows, width), bf16),
        pltpu.VMEM((3, rows, width), bf16),
        pltpu.VMEM((2, rows, width), bf16),
        pltpu.VMEM((2, rows, width), bf16),
        dma((4,)),
        dma((2, CHUNKS)),
        dma((LINE, CHUNKS)),
        dma((CHUNKS,)),
        dma((LINE,)),
        dma((LINE,)),
        dma((4,)),
        dma((LINE,)),
        dma((LINE,)),
        dma((LINE,)),
        dma((5, UNIT_CHUNKS)),
        dma((LINE, UNIT_CHUNKS)),
        dma(()),
        dma(()),
        dma((3,)),
        dma((3,)),
        dma((2,)),
        dma((2,)),
    ]


def hand_over(loss, net_grad, img_grad, loss_out, net_out, img_out, sem):
    copies = [
        pltpu.make_async_copy(src, dst, sem.at[i])
        for i, (src, dst) in enumerate(
            ((loss, loss_out), (net_grad, net_out), (img_grad, img_out))
        )
    ]
    for copy in copies:
        copy.start()
    for copy in copies:
        copy.wait()


def per_device(part_emb, assign, images, negatives):
    rows, width = images.shape
    part_rows = part_emb.shape[0]
    net_size = lax.axis_size("net")
    dp_size = lax.axis_size("dp")
    chips = net_size // 2
    pair_dp = rows * net_size
    columns = rows * dp_size
    f32, bf16 = jnp.float32, jnp.bfloat16
    dma = pltpu.SemaphoreType.DMA
    vmem = pl.BlockSpec(memory_space=pltpu.VMEM)
    hbm = pl.BlockSpec(memory_space=pltpu.HBM)
    results = (
        jax.ShapeDtypeStruct((1, rows), f32),
        jax.ShapeDtypeStruct((rows, width), f32),
        jax.ShapeDtypeStruct((rows, width), f32),
    )
    scratch = [
        pltpu.VMEM((rows, width), bf16),
        pltpu.SMEM(negatives.shape, jnp.int32),
        pltpu.VMEM((net_size, part_rows, width), bf16),
        pltpu.VMEM((net_size, 1, part_rows), jnp.int32),
        pltpu.VMEM((dp_size, rows, width), bf16),
        pltpu.VMEM((pair_dp, width), f32),
        pltpu.VMEM((pair_dp, 1), f32),
        pltpu.VMEM((pair_dp, width), bf16),
        pltpu.VMEM((columns, pair_dp), f32),
        pltpu.VMEM((columns, pair_dp), bf16),
        pltpu.VMEM((net_size, 1, pair_dp), f32),
        pltpu.VMEM((1, pair_dp), f32),
        pltpu.VMEM((net_size, rows, width), bf16),
        pltpu.VMEM((net_size, rows, width), bf16),
        pltpu.VMEM((dp_size, rows, width), bf16),
        pltpu.VMEM((dp_size, rows, width), bf16),
        dma((4,)),
        dma((chips, CHUNKS)),
        dma((net_size, CHUNKS)),
        dma((chips, CHUNKS)),
        dma((net_size,)),
        dma((net_size,)),
        dma((dp_size,)),
        dma((dp_size,)),
        dma((net_size,)),
        dma((net_size,)),
        dma((net_size,)),
        dma((net_size,)),
        dma((dp_size,)),
        dma((dp_size,)),
        pltpu.VMEM((rows, width), f32),
        pltpu.VMEM((rows, width), bf16),
        dma(()),
        dma(()),
    ]
    body = functools.partial(kernel, net_size, dp_size)
    if net_size == LINE and dp_size == LINE and rows == BLOCK:
        scratch = line_scratch(part_rows, width, negatives)
        body = line_kernel
    loss, net_grad, img_grad = pl.pallas_call(
        body,
        out_shape=results,
        in_specs=[hbm, hbm, hbm, hbm],
        out_specs=(vmem, vmem, vmem),
        scratch_shapes=scratch,
        compiler_params=pltpu.CompilerParams(
            collective_id=0, has_side_effects=True, vmem_limit_bytes=48 * 2**20
        ),
    )(*(
        pltpu.with_memory_space_constraint(array, pltpu.HBM)
        for array in (part_emb, assign.reshape(1, part_rows), images, negatives)
    ))
    loss, net_grad, img_grad = pl.pallas_call(
        hand_over,
        out_shape=results,
        in_specs=[vmem] * 3,
        out_specs=(hbm, hbm, hbm),
        scratch_shapes=[dma((3,))],
    )(*(
        pltpu.with_memory_space_constraint(array, pltpu.VMEM)
        for array in (loss, net_grad, img_grad)
    ))
    return loss.reshape(rows), net_grad, img_grad


def solution(mesh):
    in_specs = (
        P(("groups", "dp", "net"), None),
        P(("groups", "dp", "net")),
        P(("groups", "dp", "net"), None),
        P("groups", None),
    )
    out_specs = (
        P(("groups", "dp", "net")),
        P(("groups", "dp", "net"), None),
        P(("groups", "dp", "net"), None),
    )
    return jax.shard_map(
        per_device, mesh=mesh, in_specs=in_specs, out_specs=out_specs, check_vma=False
    )
```
